128 devices in a mesh: dist: 16 (over x, z_hi, core), mem: 8 (over z_lo, y).
Axes of the slice: x: 4, y: 4, z: 4 (z_hi: 2, z_lo: 2; z = z_hi * 2 + z_lo), core: 2. Of those that a mesh axis runs over, the one named last changes fastest.
Arguments:
- anomalies: bfloat16 [128, 2048, 1024], P('dist', None, 'mem'), may hold values from -6 to 6
- innovations: bfloat16 [128, 256, 1024], P('dist', None, 'mem'), may hold values from -6 to 6
- obs_var: bfloat16 [128, 256], P('dist'), may hold values from 0.25 to 2
- node_pos: bfloat16 [2, 128, 2048], P(None, 'dist'), may hold values from 0 to 1
- obs_node: int32 [128, 256], P('dist'), may hold values from 0 to 2047
- obs_count: int32 [128], P('dist'), may hold values from 64 to 256, as said below
- in_radius: int32 [128, 7], P('dist'), may hold values from 0 to 1, as said below
Outputs:
- increment: float32 [128, 2048, 1024], P('dist', 'mem')
The draws below stay inside these ranges and needn't reach their ends.
Inputs may be any that keep to these rules, and one draw needn't show every extreme that they name: `obs_count`: every district has at least 64 observations in use, and some district has all 256. `in_radius`: slot 3 (the district itself) is always 1; the ones of a district form a band of slots around it; slots naming a district outside 0 to 127 are 0; some district is paired with all districts up to 3 away.
All inputs are finite; a program needn't handle non-finite values.
Results may differ from the reference program's by a relative error of at most 0.0029.
Values may be sent and summed in bfloat16 or wider, within the bound.
A program may use at most 192 MiB of HBM per device.

```python
import math
import jax
import jax.numpy as jnp
from jax import lax

NODES = 2048
OBS_CAP = 256
RADIUS = 3
MEMBERS = 1024
DISTRICTS = 128


def draw_obs_count(key, part):
    key_counts, key_top = jax.random.split(jax.random.fold_in(key, 11))
    counts = jax.random.randint(key_counts, (DISTRICTS,), OBS_CAP // 4, OBS_CAP + 1, dtype=jnp.int32)
    top_district = jax.random.randint(key_top, (), 0, DISTRICTS, dtype=jnp.int32)
    return counts.at[top_district].set(OBS_CAP)


def draw_in_radius(key, part):
    key_first, key_second, key_top = jax.random.split(jax.random.fold_in(key, 23), 3)
    first_reach = jax.random.randint(key_first, (DISTRICTS,), 0, RADIUS + 1, dtype=jnp.int32)
    second_reach = jax.random.randint(key_second, (DISTRICTS,), 0, RADIUS + 1, dtype=jnp.int32)
    reach = jnp.minimum(first_reach, second_reach)
    top_district = jax.random.randint(key_top, (), 0, DISTRICTS, dtype=jnp.int32)
    reach = reach.at[top_district].set(RADIUS)
    offsets = jnp.arange(2 * RADIUS + 1, dtype=jnp.int32) - RADIUS
    partner = jnp.arange(DISTRICTS, dtype=jnp.int32)[:, None] + offsets[None, :]
    inside = (jnp.abs(offsets)[None, :] <= reach[:, None]) & (partner >= 0) & (partner < DISTRICTS)
    return inside.astype(jnp.int32)


def with_ends(array, stream_key, smallest, largest):
    dims = array.shape
    spot = [jax.random.randint(jax.random.fold_in(stream_key, axis), (), 0, dims[axis]) for axis in range(len(dims))]
    array = array.at[tuple(spot)].set(smallest)
    longest = dims.index(max(dims))
    spot[longest] = (spot[longest] + 1) % dims[longest]
    return array.at[tuple(spot)].set(largest)


def levels(own_key, extent, cuts, smallest, top_value):
    level, own = 1.0, jax.random.fold_in(own_key, 6)
    for dim, shards_of in cuts:
        heights = jnp.exp(jax.random.uniform(jax.random.fold_in(own, dim), (shards_of,), jnp.float32, smallest / len(cuts), top_value / len(cuts)))
        level = level * jnp.repeat(heights, extent[dim] // shards_of).reshape([-1 if axis == dim else 1 for axis in range(len(extent))])
    return level


def scatter_about(stream_key, extent, scale, most, cuts=(), held_as=jnp.bfloat16):
    level = levels(stream_key, extent, cuts, -0.22, 0.18) if cuts else 1.0
    result = jax.random.normal(stream_key, extent, jnp.float32) * scale * level
    return jnp.minimum(jnp.maximum(result, -most), most).astype(held_as)


def setup_inputs(seed: int = 0) -> dict:
    streams_of = jax.random.split(jax.random.key(seed), 8)
    anomalies = scatter_about(streams_of[0], (DISTRICTS, NODES, MEMBERS), 1.0, 6.0, ((0, 16), (2, 8)))
    innovations = scatter_about(streams_of[1], (DISTRICTS, OBS_CAP, MEMBERS), 1.0, 6.0, ((0, 16), (2, 8)))
    obs_var = jnp.clip(jnp.exp(math.log(2.0) - 2.0794415 * jax.random.uniform(streams_of[2], (DISTRICTS, OBS_CAP), jnp.float32) ** levels(streams_of[2], (DISTRICTS, OBS_CAP), ((0, 16),), -0.2, 0.2)), 0.25, 2.0).astype(jnp.bfloat16)
    node_pos = jnp.clip(1.0 * jax.random.uniform(streams_of[3], (2, DISTRICTS, NODES), jnp.float32) ** levels(streams_of[3], (2, DISTRICTS, NODES), ((1, 16),), -0.2, 0.2), 0.0, 1.0).astype(jnp.bfloat16)
    obs_node = with_ends(jax.random.randint(streams_of[4], (DISTRICTS, OBS_CAP), 0, NODES), jax.random.fold_in(streams_of[4], 1), 0, NODES - 1).astype(jnp.int32)
    obs_count = draw_obs_count(jax.random.fold_in(streams_of[7], 71), 0)
    in_radius = draw_in_radius(jax.random.fold_in(streams_of[7], 71), 0)
    return dict(anomalies=anomalies, innovations=innovations, obs_var=obs_var, node_pos=node_pos, obs_node=obs_node, obs_count=obs_count, in_radius=in_radius)


def gc_taper(ratio):
    square = ratio * ratio
    cubed = square * ratio
    fourth = cubed * ratio
    fifth_power = fourth * ratio
    inner_part = -0.25 * fifth_power + 0.5 * fourth + 0.625 * cubed - 5.0 / 3.0 * square + 1.0
    clipped = jnp.maximum(ratio, 1.0)
    outer_part = fifth_power / 12.0 - 0.5 * fourth + 0.625 * cubed + 5.0 / 3.0 * square - 5.0 * ratio + 4.0 - 2.0 / (3.0 * clipped)
    return jnp.where(ratio < 1.0, inner_part, jnp.where(ratio < 2.0, outer_part, 0.0))

def pair_gain(x_rows, obs_rows, node_xy, obs_xy, spread_row, offset, members):
    node_xy = node_xy.astype(jnp.float32)
    obs_xy = obs_xy.astype(jnp.float32)
    delta_x = offset + obs_xy[0][None, :] - node_xy[0][:, None]
    delta_y = obs_xy[1][None, :] - node_xy[1][:, None]
    distance = jnp.sqrt(delta_x * delta_x + delta_y * delta_y)
    weight = gc_taper(distance / ((RADIUS + 2) / 2.0))
    covariance = lax.dot_general(x_rows, obs_rows, (((1,), (1,)), ((), ())), preferred_element_type=jnp.float32) / (members - 1)
    return (weight * covariance / spread_row[None, :]).astype(jnp.bfloat16)

def pick_rows(table, index):
    return table[index]

def pick_columns(table, index):
    return table[:, index]

def reference(anomalies, innovations, obs_var, node_pos, obs_node, obs_count, in_radius):
    members = anomalies.shape[2]
    live_slot = jnp.arange(OBS_CAP, dtype=jnp.int32)[None, :] < obs_count[:, None]
    picked = jax.vmap(pick_rows)(anomalies, obs_node)
    observed = jnp.where(live_slot[:, :, None], picked, jnp.zeros((), jnp.bfloat16))
    obs_xy = jax.vmap(pick_columns, in_axes=(1, 0), out_axes=1)(node_pos, obs_node)
    spread = lax.optimization_barrier(jnp.sum(jnp.square(observed.astype(jnp.float32)), axis=2)) / (members - 1) + obs_var.astype(jnp.float32)

    def one_district(district):
        x_rows = lax.dynamic_index_in_dim(anomalies, district, 0, keepdims=False)
        node_xy = lax.dynamic_index_in_dim(node_pos, district, 1, keepdims=False)
        total = jnp.zeros((NODES, members), jnp.float32)
        for slot in range(2 * RADIUS + 1):
            other = jnp.clip(district + slot - RADIUS, 0, DISTRICTS - 1).astype(jnp.int32)

            def accumulate(current, other=other, slot=slot):
                obs_rows = lax.dynamic_index_in_dim(observed, other, 0, keepdims=False)
                innov_rows = lax.dynamic_index_in_dim(innovations, other, 0, keepdims=False)
                partner_xy = lax.dynamic_index_in_dim(obs_xy, other, 1, keepdims=False)
                spread_row = lax.dynamic_index_in_dim(spread, other, 0, keepdims=False)
                gain = pair_gain(x_rows, obs_rows, node_xy, partner_xy, spread_row, float(slot - RADIUS), members)
                return current + jnp.dot(gain, innov_rows, preferred_element_type=jnp.float32)

            def unchanged(current):
                return current
            flag = lax.dynamic_index_in_dim(lax.dynamic_index_in_dim(in_radius, district, 0, keepdims=False), slot, 0, keepdims=False)
            total = lax.cond(flag > 0, accumulate, unchanged, total)
        return total
    return lax.map(one_district, jnp.arange(DISTRICTS, dtype=jnp.int32))
```

```python
import functools
import jax
import jax.numpy as jnp
from jax import lax
from jax.experimental import pallas as pl
from jax.experimental.pallas import tpu as pltpu
from jax.sharding import PartitionSpec as P

MESH = pl.DeviceIdType.MESH
ANY = pl.BlockSpec(memory_space=pl.ANY)
VMEM = pl.BlockSpec(memory_space=pltpu.VMEM)
SMEM = pl.BlockSpec(memory_space=pltpu.SMEM)
DMA = pltpu.SemaphoreType.DMA
RADIUS = 3
REACH = 2.5


def prep_kernel(count_ref, anom_ref, innov_ref, node_ref, pos_ref, var_ref, src_ref, meta_ref, cols):
    d = pl.program_id(0)

    @pl.when(d == 0)
    def _():
        cols[...] = node_ref[...].T

    lane = lax.broadcasted_iota(jnp.int32, (256, 8), 1)
    node = jnp.sum(jnp.where(lane == d, cols[...], 0), axis=1, keepdims=True)
    slot = lax.broadcasted_iota(jnp.int32, (256, 1), 0)
    node = jnp.where(slot < count_ref[d], node, -1)
    hot = jnp.where(lax.broadcasted_iota(jnp.int32, (256, 2048), 1) == node, 1.0, 0.0).astype(jnp.bfloat16)
    src_ref[0, 0] = jnp.dot(hot, anom_ref[0], preferred_element_type=jnp.float32).astype(jnp.bfloat16)
    src_ref[1, 0] = innov_ref[0]
    spots = lax.dot_general(pos_ref[...], hot, (((1,), (1,)), ((), ())), preferred_element_type=jnp.float32)
    row16 = lax.broadcasted_iota(jnp.int32, (16, 256), 0)
    row8 = lax.broadcasted_iota(jnp.int32, (8, 256), 0)
    x = jnp.sum(jnp.where(row16 == d, spots, 0.0), axis=0, keepdims=True)
    yy = jnp.sum(jnp.where(row16 == d + 8, spots, 0.0), axis=0, keepdims=True)
    var = jnp.sum(jnp.where(row8 == d, var_ref[...].astype(jnp.float32), 0.0), axis=0, keepdims=True)
    meta_ref[0] = jnp.where(row8 == 0, x, jnp.where(row8 == 1, yy, jnp.where(row8 == 2, var, 0.0)))


def prep(anomalies, innovations, obs_var, node_pos, obs_node, obs_count):
    return pl.pallas_call(
        prep_kernel,
        grid=(8,),
        out_shape=(jax.ShapeDtypeStruct((2, 8, 256, 128), jnp.bfloat16), jax.ShapeDtypeStruct((8, 8, 256), jnp.float32)),
        in_specs=[
            SMEM,
            pl.BlockSpec((1, 2048, 128), lambda d: (d, 0, 0)),
            pl.BlockSpec((1, 256, 128), lambda d: (d, 0, 0)),
            VMEM,
            VMEM,
            VMEM,
        ],
        out_specs=(pl.BlockSpec((2, 1, 256, 128), lambda d: (0, d, 0, 0)), pl.BlockSpec((1, 8, 256), lambda d: (d, 0, 0))),
        scratch_shapes=[pltpu.VMEM((256, 8), jnp.int32)],
        compiler_params=pltpu.CompilerParams(vmem_limit_bytes=24 << 20),
    )(obs_count, anomalies, innovations, obs_node, node_pos.reshape(16, 2048), obs_var)


def exchange_kernel(anom, src, meta, xo, oi, mo, a_s, a_r, g_s, g_r, h_s, h_r, m_s, m_r, l_s):
    di, j = lax.axis_index("dist"), lax.axis_index("mem")
    core = lax.rem(di, 2)
    zl, y = j // 4, lax.rem(j, 4)

    def mem_of(z, row):
        return z * 4 + lax.rem(row + 8, 4)

    flip = mem_of(1 - zl, y)
    other = di + 1 - 2 * core
    remote = lax.rem(di + 15 + 2 * core, 16)
    barrier = pltpu.get_barrier_semaphore()
    for k in range(1, 8):
        pl.semaphore_signal(barrier, inc=1, device_id={"dist": di, "mem": lax.rem(j + k, 8)}, device_id_type=MESH)
    pl.semaphore_signal(barrier, inc=1, device_id={"dist": other, "mem": j}, device_id_type=MESH)
    pl.semaphore_signal(barrier, inc=1, device_id={"dist": remote, "mem": flip}, device_id_type=MESH)
    pl.semaphore_wait(barrier, 9)

    def remote_copy(source, target, send, recv, dist, mem):
        return pltpu.make_async_remote_copy(
            src_ref=source, dst_ref=target, send_sem=send, recv_sem=recv,
            device_id={"dist": dist, "mem": mem}, device_id_type=MESH)

    own_src = pltpu.make_async_copy(src, oi.at[:, pl.ds(3, 8), j], l_s.at[0])
    own_x = pltpu.make_async_copy(anom.at[:, pl.ds(pl.multiple_of(j * 256, 256), 256), :], xo.at[:, j], l_s.at[1])
    own_meta = pltpu.make_async_copy(meta, mo.at[pl.ds(3, 8)], l_s.at[2])
    own_src.start()
    own_x.start()
    own_meta.start()
    near_first = core == 1
    to_prev = remote_copy(
        meta.at[pl.ds(0, 3)], mo.at[pl.ds(11, 3)], m_s.at[0], m_r.at[0],
        jnp.where(near_first, other, remote), jnp.where(near_first, j, flip))
    to_next = remote_copy(
        meta.at[pl.ds(5, 3)], mo.at[pl.ds(0, 3)], m_s.at[1], m_r.at[1],
        jnp.where(near_first, remote, other), jnp.where(near_first, flip, j))
    to_prev.start()
    to_next.start()

    def a_copy(k, d):
        target = mem_of(lax.rem(zl + k // 4, 2), y + k % 4)
        return remote_copy(
            anom.at[d, pl.ds(pl.multiple_of(target * 256, 256), 256), :], xo.at[d, j],
            a_s.at[k - 1, d], a_r.at[k - 1, d], di, target)

    def unit(u):
        q = lax.rem(u, 8)
        return u // 8, q, q + core * (7 - 2 * q), 1 - 2 * lax.rem(u, 2)

    def own(u, edge):
        kind, q, d, s = unit(u)
        target = (mem_of(zl, y + s), mem_of(zl, y - s), flip)[edge]
        return remote_copy(src.at[kind, d], oi.at[kind, 3 + d, j], g_s.at[edge, u], g_r.at[edge, u], di, target)

    def forward(u, edge):
        kind, q, d, s = unit(u)
        held, target = {
            3: (mem_of(zl, y - s), flip),
            4: (mem_of(zl, y + s), mem_of(zl, y - s)),
            5: (flip, mem_of(zl, y - s)),
            6: (mem_of(1 - zl, y - s), mem_of(zl, y + s)),
        }[edge]
        block = oi.at[kind, 3 + d, held]
        return remote_copy(block, block, g_s.at[edge, u], g_r.at[edge, u], di, target)

    def gathered(u, edge):
        kind, q, d, s = unit(u)
        block = oi.at[kind, 3 + d, {
            0: mem_of(zl, y - s),
            1: mem_of(zl, y + s),
            2: flip,
            3: mem_of(1 - zl, y - s),
            4: mem_of(zl, y + 2),
            5: mem_of(1 - zl, y + s),
            6: mem_of(1 - zl, y + 2),
        }[edge]]
        return remote_copy(block, block, g_s.at[edge, u], g_r.at[edge, u], di, flip)

    def halo(u):
        kind, q, d, s = unit(u)
        near = q >= 5
        slot = jnp.where(d >= 5, d - 5, 11 + d)
        index = jnp.where(near, q - 2, q)
        return remote_copy(
            oi.at[kind, 3 + d], oi.at[kind, slot], h_s.at[kind, index], h_r.at[kind, index],
            jnp.where(near, other, remote), jnp.where(near, j, flip))

    def halo_in(kind, index):
        slot = jnp.where(core == 0, jnp.where(index < 3, 2 - index, 16 - index), jnp.where(index < 3, 11 + index, index - 3))
        return remote_copy(oi.at[kind, slot], oi.at[kind, slot], h_s.at[kind, index], h_r.at[kind, index], other, j)

    own_src.wait()

    def step(t, carry):
        @pl.when(t < 16)
        def _():
            for edge in range(3):
                own(t, edge).start()

        @pl.when((t < 16) & (lax.rem(t, 2) == 0))
        def _():
            for k in (6, 2, 5, 7, 4, 1, 3):
                a_copy(k, t // 2).start()

        u = t - 1

        @pl.when((u >= 0) & (u < 16))
        def _():
            for edge in range(3):
                gathered(u, edge).wait_recv()
                forward(u, edge + 3).start()

        v = t - 2

        @pl.when((v >= 0) & (v < 16))
        def _():
            gathered(v, 3).wait_recv()
            forward(v, 6).start()

        w = t - 3

        @pl.when((w >= 0) & (w < 16))
        def _():
            for edge in (4, 5, 6):
                gathered(w, edge).wait_recv()
            q = lax.rem(w, 8)

            @pl.when((q < 3) | (q >= 5))
            def _():
                halo(w).start()

        return carry

    lax.fori_loop(0, 19, step, 0)

    def drain(u, carry):
        for edge in range(7):
            gathered(u, edge).wait_send()
        q = lax.rem(u, 8)

        @pl.when((q < 3) | (q >= 5))
        def _():
            halo(u).wait_send()
            halo_in(u // 8, jnp.where(q >= 5, q - 2, q)).wait_recv()

        return carry

    lax.fori_loop(0, 16, drain, 0)

    def a_drain(d, carry):
        for k in range(1, 8):
            a_copy(k, d).wait_send()
            source = mem_of(lax.rem(zl + k // 4, 2), y + 4 - k % 4)
            block = xo.at[d, source]
            remote_copy(block, block, a_s.at[k - 1, d], a_r.at[k - 1, d], di, flip).wait_recv()
        return carry

    lax.fori_loop(0, 8, a_drain, 0)
    own_x.wait()
    own_meta.wait()
    to_prev.wait()
    to_next.wait()


def exchange(anom, src, meta):
    return pl.pallas_call(
        exchange_kernel,
        out_shape=(
            jax.ShapeDtypeStruct((8, 8, 256, 128), jnp.bfloat16),
            jax.ShapeDtypeStruct((2, 14, 8, 256, 128), jnp.bfloat16),
            jax.ShapeDtypeStruct((14, 8, 256), jnp.float32),
        ),
        in_specs=[ANY, ANY, ANY],
        out_specs=(ANY, ANY, ANY),
        scratch_shapes=[
            DMA((7, 8)), DMA((7, 8)), DMA((7, 16)), DMA((7, 16)), DMA((2, 6)), DMA((2, 6)), DMA((2,)), DMA((2,)), DMA((3,))],
        compiler_params=pltpu.CompilerParams(collective_id=0, has_side_effects=True, vmem_limit_bytes=8 << 20),
    )(anom, src, meta)


def pair_gain(cov, node_xy, meta, inv, shift):
    dx = (meta[0:1] + shift) - node_xy[:, 0:1]
    dy = meta[1:2] - node_xy[:, 1:2]
    square = jnp.maximum((dx * dx + dy * dy) * (1.0 / (REACH * REACH)), 1e-30)
    root = lax.rsqrt(square)
    z = square * root
    inner = (((-0.25 * z + 0.5) * z + 0.625) * z - 5.0 / 3.0) * square + 1.0
    left = jnp.maximum(2.0 - z, 0.0)
    left = left * left
    outer = (left * left) * (z * (1.0 / 12.0) + (1.0 / 6.0) - root * (1.0 / 24.0))
    return (jnp.where(z < 1.0, inner, outer) * cov * inv).astype(jnp.bfloat16)


def analysis_kernel(flag_ref, x_ref, xy_ref, meta_ref, oi_hbm, out_ref, oi, inv, cov, gain, sem):
    d = pl.program_id(0)

    def fetch(kind, e):
        return pltpu.make_async_copy(oi_hbm.at[kind, e], oi.at[kind, e], sem.at[kind, e])

    @pl.when(d == 0)
    def _():
        for e in range(14):
            for kind in range(2):
                fetch(kind, e).start()

    def full(kind, e):
        return jnp.concatenate([oi[kind, e, j] for j in range(8)], axis=1)

    def arrive(e):
        fetch(0, e).wait()
        fetch(1, e).wait()
        obs = full(0, e)
        gram = lax.dot_general(obs, obs, (((1,), (1,)), ((), ())), preferred_element_type=jnp.float32)
        same = lax.broadcasted_iota(jnp.int32, (256, 256), 0) == lax.broadcasted_iota(jnp.int32, (256, 256), 1)
        total = jnp.sum(jnp.where(same, gram, 0.0), axis=0, keepdims=True)
        inv[pl.ds(e, 1)] = 1.0 / (total + 1023.0 * meta_ref[e, 2:3])

    @pl.when(d == 0)
    def _():
        def one(e, c):
            arrive(e)
            return c
        lax.fori_loop(0, 7, one, 0)

    @pl.when(d > 0)
    def _():
        arrive(d + 6)

    def pair(s):
        e = d + s
        x = jnp.concatenate([x_ref[0, j] for j in range(8)], axis=1)
        cov[...] = lax.dot_general(x, full(0, e), (((1,), (1,)), ((), ())), preferred_element_type=jnp.float32)
        meta, row = meta_ref[e], inv[pl.ds(e, 1)]
        shift = (s - RADIUS).astype(jnp.float32)

        def rows(i, c):
            r = pl.ds(pl.multiple_of(i * 32, 32), 32)
            gain[r] = pair_gain(cov[r], xy_ref[0, r], meta, row, shift)
            return c

        lax.fori_loop(0, 8, rows, 0)
        return jnp.dot(gain[...], full(1, e), preferred_element_type=jnp.float32)

    out_ref[0] = pair(jnp.int32(RADIUS))

    def slots(s, c):
        @pl.when((s != RADIUS) & (flag_ref[d, s] > 0))
        def _():
            out_ref[0] += pair(s)
        return c

    lax.fori_loop(0, 7, slots, 0)


def analysis(in_radius, xs, own_xy, meta, oi):
    return pl.pallas_call(
        analysis_kernel,
        grid=(8,),
        out_shape=jax.ShapeDtypeStruct((8, 256, 1024), jnp.float32),
        in_specs=[
            SMEM,
            pl.BlockSpec((1, 8, 256, 128), lambda d: (d, 0, 0, 0)),
            pl.BlockSpec((1, 256, 2), lambda d: (d, 0, 0)),
            VMEM,
            ANY,
        ],
        out_specs=pl.BlockSpec((1, 256, 1024), lambda d: (d, 0, 0)),
        scratch_shapes=[
            pltpu.VMEM((2, 14, 8, 256, 128), jnp.bfloat16),
            pltpu.VMEM((14, 256), jnp.float32),
            pltpu.VMEM((256, 256), jnp.float32),
            pltpu.VMEM((256, 256), jnp.bfloat16),
            DMA((2, 14)),
        ],
        compiler_params=pltpu.CompilerParams(vmem_limit_bytes=40 << 20),
    )(in_radius, xs, own_xy, meta, oi)


def on_device(anomalies, innovations, obs_var, node_pos, obs_node, obs_count, in_radius):
    src, meta = prep(anomalies, innovations, obs_var, node_pos, obs_node, obs_count)
    own_xy = lax.dynamic_slice_in_dim(node_pos, lax.axis_index("mem") * 256, 256, 2)
    own_xy = jnp.transpose(own_xy, (1, 2, 0)).astype(jnp.float32)
    xs, oi, meta = exchange(anomalies, src, meta)
    return analysis(in_radius, xs, own_xy, meta, oi)


def solution(mesh):
    return jax.shard_map(
        on_device,
        mesh=mesh,
        in_specs=(
            P("dist", None, "mem"),
            P("dist", None, "mem"),
            P("dist", None),
            P(None, "dist", None),
            P("dist", None),
            P("dist"),
            P("dist", None),
        ),
        out_specs=P("dist", "mem", None),
        check_vma=False,
    )
```

```python
import jax
import jax.numpy as jnp
from jax import lax
from jax.experimental import pallas as pl
from jax.experimental.pallas import tpu as pltpu
from jax.sharding import PartitionSpec as P

MESH = pl.DeviceIdType.MESH
HBM = pl.BlockSpec(memory_space=pltpu.HBM)
VMEM = pl.BlockSpec(memory_space=pltpu.VMEM)
SMEM = pl.BlockSpec(memory_space=pltpu.SMEM)
DMA = pltpu.SemaphoreType.DMA
RADIUS = 3
REACH = 2.5
UNITS = 16
LAG = 2
FAR_FIRST = (6, 2, 5, 7, 4, 1, 3)


def exchange_kernel(
    anom, innov, node_h, count_h, pos_h, var_h, xo, oi, mo, xy_o,
    held, seen, meta, xy, node, count, pos, var, cols,
    a_s, a_r, g_s, g_r, h_s, h_r, m_s, m_r, l_s, p_s, w_s,
):
    di, j = lax.axis_index("dist"), lax.axis_index("mem")
    core = lax.rem(di, 2)
    zl, y = j // 4, lax.rem(j, 4)

    def mem_of(z, row):
        return z * 4 + lax.rem(row + 8, 4)

    def district(q):
        return q + core * (7 - 2 * q)

    small = [
        pltpu.make_async_copy(node_h, node, l_s.at[0]),
        pltpu.make_async_copy(count_h, count, l_s.at[1]),
        pltpu.make_async_copy(pos_h, pos, l_s.at[2]),
        pltpu.make_async_copy(var_h, var, l_s.at[3]),
    ]
    for copy in small:
        copy.start()

    def load(q):
        return pltpu.make_async_copy(anom.at[district(q)], held.at[lax.rem(q, 2)], p_s.at[lax.rem(q, 2)])

    load(0).start()
    load(1).start()
    own_x = pltpu.make_async_copy(anom.at[:, pl.ds(pl.multiple_of(j * 256, 256), 256), :], xo.at[:, j], l_s.at[4])
    own_innov = pltpu.make_async_copy(innov, oi.at[1, pl.ds(3, 8), j], l_s.at[5])
    own_x.start()
    own_innov.start()

    flip = mem_of(1 - zl, y)
    other = di + 1 - 2 * core
    remote = lax.rem(di + 15 + 2 * core, 16)
    barrier = pltpu.get_barrier_semaphore()
    for k in range(1, 8):
        pl.semaphore_signal(barrier, inc=1, device_id={"dist": di, "mem": lax.rem(j + k, 8)}, device_id_type=MESH)
    pl.semaphore_signal(barrier, inc=1, device_id={"dist": other, "mem": j}, device_id_type=MESH)
    pl.semaphore_signal(barrier, inc=1, device_id={"dist": remote, "mem": flip}, device_id_type=MESH)
    pl.semaphore_wait(barrier, 9)

    def remote_copy(source, target, send, recv, dist, mem):
        return pltpu.make_async_remote_copy(
            src_ref=source, dst_ref=target, send_sem=send, recv_sem=recv,
            device_id={"dist": dist, "mem": mem}, device_id_type=MESH)

    def spread_nodes(k, q):
        d = district(q)
        target = mem_of(lax.rem(zl + k // 4, 2), y + k % 4)
        return remote_copy(
            anom.at[d, pl.ds(pl.multiple_of(target * 256, 256), 256), :], xo.at[d, j],
            a_s.at[k - 1, q], a_r.at[k - 1, q], di, target)

    def unit(u):
        early = u < 6
        kind = jnp.where(early, u // 3, (u - 6) // 5)
        q = jnp.where(early, lax.rem(u, 3), 3 + lax.rem(u + 4, 5))
        return kind, q, district(q), 1 - 2 * lax.rem(u, 2), lax.rem(u, 3) == 2

    def edge_copy(u, edge, source, block, mem):
        return remote_copy(source, block, g_s.at[edge, u], g_r.at[edge, u], di, mem)

    def forward(u, edge):
        kind, q, d, s, three = unit(u)
        here, there = zl, 1 - zl
        from_, to = {
            3: (mem_of(here, y - s), flip),
            4: (mem_of(here, y + s), jnp.where(three, flip, mem_of(here, y - s))),
            5: (jnp.where(three, mem_of(here, y - s), flip), jnp.where(three, mem_of(here, y + s), mem_of(here, y - s))),
            6: (jnp.where(three, mem_of(there, y + s), mem_of(there, y - s)),
                jnp.where(three, mem_of(here, y - s), mem_of(here, y + s))),
        }[edge]
        block = oi.at[kind, 3 + d, from_]
        return edge_copy(u, edge, block, block, to)

    def gathered(u, edge):
        kind, q, d, s, three = unit(u)
        here, there = zl, 1 - zl
        from_ = (
            mem_of(here, y - s),
            mem_of(here, y + s),
            flip,
            mem_of(there, y - s),
            jnp.where(three, mem_of(there, y + s), mem_of(here, y + 2)),
            jnp.where(three, mem_of(here, y + 2), mem_of(there, y + s)),
            mem_of(there, y + 2),
        )[edge]
        block = oi.at[kind, 3 + d, from_]
        return edge_copy(u, edge, block, block, flip)

    def halo(u):
        kind, q, d, s, three = unit(u)
        near = q >= 5
        slot = jnp.where(d >= 5, d - 5, 11 + d)
        index = jnp.where(near, q - 2, q)
        return remote_copy(
            oi.at[kind, 3 + d], oi.at[kind, slot], h_s.at[kind, index], h_r.at[kind, index],
            jnp.where(near, other, remote), jnp.where(near, j, flip))

    def halo_in(kind, index):
        slot = jnp.where(core == 0, jnp.where(index < 3, 2 - index, 16 - index), jnp.where(index < 3, 11 + index, index - 3))
        return remote_copy(oi.at[kind, slot], oi.at[kind, slot], h_s.at[kind, index], h_r.at[kind, index], other, j)

    def has_halo(u):
        q = unit(u)[1]
        return (q < 3) | (q >= 5)

    def own_seen(d):
        return pltpu.make_async_copy(seen.at[d], oi.at[0, 3 + d, j], w_s.at[d])

    for k in FAR_FIRST:
        spread_nodes(k, 0).start()
    for copy in small:
        copy.wait()
    slot8 = lax.broadcasted_iota(jnp.int32, (256, 8), 0)
    cols[...] = jnp.where(slot8 < count[...], node[...].T, -1)
    xy[...] = pos[:, pl.ds(pl.multiple_of(j * 256, 256), 256)].astype(jnp.float32).T

    def observe(q):
        d = district(q)
        load(q).wait()
        lane = lax.broadcasted_iota(jnp.int32, (256, 8), 1)
        which = jnp.sum(jnp.where(lane == d, cols[...], 0), axis=1, keepdims=True)
        hot = jnp.where(lax.broadcasted_iota(jnp.int32, (256, 2048), 1) == which, 1.0, 0.0).astype(jnp.bfloat16)
        rows = jnp.dot(hot, held[lax.rem(q, 2)], preferred_element_type=jnp.float32)
        seen[d] = rows.astype(jnp.bfloat16)
        spots = lax.dot_general(pos[...], hot, (((1,), (1,)), ((), ())), preferred_element_type=jnp.float32)
        row16 = lax.broadcasted_iota(jnp.int32, (16, 256), 0)
        row8 = lax.broadcasted_iota(jnp.int32, (8, 256), 0)
        sx = jnp.sum(jnp.where(row16 == d, spots, 0.0), axis=0, keepdims=True)
        sy = jnp.sum(jnp.where(row16 == d + 8, spots, 0.0), axis=0, keepdims=True)
        sv = jnp.sum(jnp.where(row8 == d, var[...].astype(jnp.float32), 0.0), axis=0, keepdims=True)
        meta[d] = jnp.where(row8 == 0, sx, jnp.where(row8 == 1, sy, jnp.where(row8 == 2, sv, 0.0)))

        @pl.when(q < 6)
        def _():
            load(q + 2).start()

        own_seen(d).start()

    near_first = core == 1
    to_prev = remote_copy(
        meta.at[pl.ds(0, 3)], mo.at[pl.ds(11, 3)], m_s.at[0], m_r.at[0],
        jnp.where(near_first, other, remote), jnp.where(near_first, j, flip))
    to_next = remote_copy(
        meta.at[pl.ds(5, 3)], mo.at[pl.ds(0, 3)], m_s.at[1], m_r.at[1],
        jnp.where(near_first, remote, other), jnp.where(near_first, flip, j))
    own_meta = pltpu.make_async_copy(meta, mo.at[pl.ds(3, 8)], l_s.at[0])
    own_xy = pltpu.make_async_copy(xy, xy_o, l_s.at[1])
    own_xy.start()

    def step(t, carry):
        @pl.when(t < UNITS)
        def _():
            kind, q, d, s, three = unit(t)
            targets = (mem_of(zl, y + s), mem_of(zl, y - s), flip)

            @pl.when(kind == 0)
            def _():
                observe(q)
                for edge in range(3):
                    edge_copy(t, edge, seen.at[d], oi.at[0, 3 + d, j], targets[edge]).start()

            @pl.when(kind == 1)
            def _():
                for edge in range(3):
                    edge_copy(t, edge, innov.at[d], oi.at[1, 3 + d, j], targets[edge]).start()

        @pl.when((t >= 2) & (t < UNITS) & (lax.rem(t, 2) == 0))
        def _():
            for k in FAR_FIRST:
                spread_nodes(k, t // 2).start()

        @pl.when(t == 11)
        def _():
            to_prev.start()
            to_next.start()
            own_meta.start()

        u = t - LAG

        @pl.when((u >= 0) & (u < UNITS))
        def _():
            for edge in range(3):
                gathered(u, edge).wait_recv()
                forward(u, edge + 3).start()

        v = t - 2 * LAG

        @pl.when((v >= 0) & (v < UNITS))
        def _():
            gathered_last(v, True)
            forward(v, 6).start()

        w = t - 3 * LAG

        @pl.when((w >= 0) & (w < UNITS))
        def _():
            gathered_last(w, False)
            gathered(w, 5).wait_recv()
            gathered(w, 6).wait_recv()
            kind, q, d, s, three = unit(w)

            @pl.when(kind == 0)
            def _():
                own_seen(d).wait()

            @pl.when(w == 3)
            def _():
                own_innov.wait()

            @pl.when(has_halo(w))
            def _():
                halo(w).start()

        return carry

    def gathered_last(u, first):
        three = unit(u)[4]
        take4 = three if first else jnp.logical_not(three)

        @pl.when(take4)
        def _():
            gathered(u, 4).wait_recv()

        @pl.when(jnp.logical_not(take4))
        def _():
            gathered(u, 3).wait_recv()

    lax.fori_loop(0, UNITS + 3 * LAG, step, 0)

    def drain(u, carry):
        for edge in range(7):
            gathered(u, edge).wait_send()

        @pl.when(has_halo(u))
        def _():
            kind, q, d, s, three = unit(u)
            halo(u).wait_send()
            halo_in(kind, jnp.where(q >= 5, q - 2, q)).wait_recv()

        return carry

    lax.fori_loop(0, UNITS, drain, 0)

    def drain_nodes(q, carry):
        for k in range(1, 8):
            spread_nodes(k, q).wait_send()
            source = mem_of(lax.rem(zl + k // 4, 2), y + 4 - k % 4)
            block = xo.at[district(q), source]
            remote_copy(block, block, a_s.at[k - 1, q], a_r.at[k - 1, q], di, flip).wait_recv()
        return carry

    lax.fori_loop(0, 8, drain_nodes, 0)
    own_x.wait()
    own_meta.wait()
    own_xy.wait()
    to_prev.wait()
    to_next.wait()


def exchange(anomalies, innovations, obs_var, node_pos, obs_node, obs_count):
    return pl.pallas_call(
        exchange_kernel,
        out_shape=(
            jax.ShapeDtypeStruct((8, 8, 256, 128), jnp.bfloat16),
            jax.ShapeDtypeStruct((2, 14, 8, 256, 128), jnp.bfloat16),
            jax.ShapeDtypeStruct((14, 8, 256), jnp.float32),
            jax.ShapeDtypeStruct((256, 16), jnp.float32),
        ),
        in_specs=[HBM] * 6,
        out_specs=(HBM,) * 4,
        scratch_shapes=[
            pltpu.VMEM((2, 2048, 128), jnp.bfloat16),
            pltpu.VMEM((8, 256, 128), jnp.bfloat16),
            pltpu.VMEM((8, 8, 256), jnp.float32),
            pltpu.VMEM((256, 16), jnp.float32),
            pltpu.VMEM((8, 256), jnp.int32),
            pltpu.VMEM((1, 8), jnp.int32),
            pltpu.VMEM((16, 2048), jnp.bfloat16),
            pltpu.VMEM((8, 256), jnp.bfloat16),
            pltpu.VMEM((256, 8), jnp.int32),
            DMA((7, 8)), DMA((7, 8)), DMA((7, UNITS)), DMA((7, UNITS)), DMA((2, 6)), DMA((2, 6)), DMA((2,)), DMA((2,)),
            DMA((6,)), DMA((2,)), DMA((8,)),
        ],
        compiler_params=pltpu.CompilerParams(collective_id=0, has_side_effects=True, vmem_limit_bytes=56 << 20),
    )(anomalies, innovations, obs_node, obs_count.reshape(1, 8), node_pos.reshape(16, 2048), obs_var)


def taper(node_x, node_y, meta, shift):
    dx = (meta[0:1] + shift) - node_x
    dy = meta[1:2] - node_y
    square = jnp.maximum((dx * dx + dy * dy) * (1.0 / (REACH * REACH)), 1e-30)
    root = lax.rsqrt(square)
    z = square * root
    inner = (((-0.25 * z + 0.5) * z + 0.625) * z - 5.0 / 3.0) * square + 1.0
    left = jnp.maximum(2.0 - z, 0.0)
    left = left * left
    outer = (left * left) * (z * (1.0 / 12.0) + (1.0 / 6.0) - root * (1.0 / 24.0))
    return jnp.where(z < 1.0, inner, outer)


def analysis_kernel(flag_ref, x_ref, xy_ref, meta_ref, oi_hbm, out_ref, oi, inv, cov, gain, sem):
    d = pl.program_id(0)

    def fetch(kind, e):
        return pltpu.make_async_copy(oi_hbm.at[kind, e], oi.at[kind, e], sem.at[kind, e])

    @pl.when(d == 0)
    def _():
        for e in range(14):
            for kind in range(2):
                fetch(kind, e).start()

    def full(kind, e):
        return jnp.concatenate([oi[kind, e, j] for j in range(8)], axis=1)

    def arrive(e):
        fetch(0, e).wait()
        fetch(1, e).wait()
        total = jnp.zeros((256, 128), jnp.float32)
        for j in range(8):
            part = oi[0, e, j].astype(jnp.float32)
            total = total + part * part
        total = jnp.sum(total.T, axis=0, keepdims=True)
        inv[pl.ds(e, 1)] = 1.0 / (total + 1023.0 * meta_ref[e, 2:3])

    @pl.when(d == 0)
    def _():
        def one(e, c):
            arrive(e)
            return c
        lax.fori_loop(0, 7, one, 0)

    @pl.when(d > 0)
    def _():
        arrive(d + 6)

    lane = lax.broadcasted_iota(jnp.int32, (256, 16), 1)
    node_x = jnp.sum(jnp.where(lane == d, xy_ref[...], 0.0), axis=1, keepdims=True)
    node_y = jnp.sum(jnp.where(lane == d + 8, xy_ref[...], 0.0), axis=1, keepdims=True)

    def pair(s):
        e = d + s
        x = jnp.concatenate([x_ref[0, j] for j in range(8)], axis=1)
        cov[...] = lax.dot_general(x, full(0, e), (((1,), (1,)), ((), ())), preferred_element_type=jnp.float32)
        meta, row = meta_ref[e], inv[pl.ds(e, 1)]
        shift = (s - RADIUS).astype(jnp.float32)
        for i in range(0, 256, 32):
            r = slice(i, i + 32)
            gain[r] = (taper(node_x[r], node_y[r], meta, shift) * cov[r] * row).astype(jnp.bfloat16)
        return jnp.dot(gain[...], full(1, e), preferred_element_type=jnp.float32)

    out_ref[0] = pair(jnp.int32(RADIUS))

    def slots(s, c):
        @pl.when((s != RADIUS) & (flag_ref[d, s] > 0))
        def _():
            out_ref[0] += pair(s)
        return c

    lax.fori_loop(0, 7, slots, 0)


def analysis(in_radius, xs, own_xy, meta, oi):
    return pl.pallas_call(
        analysis_kernel,
        grid=(8,),
        out_shape=jax.ShapeDtypeStruct((8, 256, 1024), jnp.float32),
        in_specs=[
            SMEM,
            pl.BlockSpec((1, 8, 256, 128), lambda d: (d, 0, 0, 0)),
            VMEM,
            VMEM,
            HBM,
        ],
        out_specs=pl.BlockSpec((1, 256, 1024), lambda d: (d, 0, 0)),
        scratch_shapes=[
            pltpu.VMEM((2, 14, 8, 256, 128), jnp.bfloat16),
            pltpu.VMEM((14, 256), jnp.float32),
            pltpu.VMEM((256, 256), jnp.float32),
            pltpu.VMEM((256, 256), jnp.bfloat16),
            DMA((2, 14)),
        ],
        compiler_params=pltpu.CompilerParams(vmem_limit_bytes=56 << 20),
    )(in_radius, xs, own_xy, meta, oi)


def on_device(anomalies, innovations, obs_var, node_pos, obs_node, obs_count, in_radius):
    xs, oi, meta, own_xy = exchange(anomalies, innovations, obs_var, node_pos, obs_node, obs_count)
    return analysis(in_radius, xs, own_xy, meta, oi)


def solution(mesh):
    return jax.shard_map(
        on_device,
        mesh=mesh,
        in_specs=(
            P("dist", None, "mem"),
            P("dist", None, "mem"),
            P("dist", None),
            P(None, "dist", None),
            P("dist", None),
            P("dist"),
            P("dist", None),
        ),
        out_specs=P("dist", "mem", None),
        check_vma=False,
    )
```

```python
import jax
import jax.numpy as jnp
from jax import lax
from jax.experimental import pallas as pl
from jax.experimental.pallas import tpu as pltpu
from jax.sharding import PartitionSpec as P

MESH = pl.DeviceIdType.MESH
HBM = pl.BlockSpec(memory_space=pltpu.HBM)
VMEM = pl.BlockSpec(memory_space=pltpu.VMEM)
SMEM = pl.BlockSpec(memory_space=pltpu.SMEM)
DMA = pltpu.SemaphoreType.DMA
RADIUS = 3
REACH = 2.5
UNITS = 16
LAG = 2
FAR_FIRST = (6, 2, 5, 7, 4, 1, 3)
STEPS = 25
X_STEP = (4, 5, 7, 8, 10, 11, 13, 14)


def column(*parts):
    items = [(e + 3) * 8 + d for e, own in parts for d in own]
    return sum(item * 128 ** i for i, item in enumerate(items))


GAIN_FIRST = 9
GAIN_TABLE = (
    column((0, (0, 1, 2, 3))),
    column((1, (0, 1, 2, 3))),
    column((1, (4,)), (-1, (0, 1, 2))),
    column((2, (0, 1, 2, 3))),
    column((2, (4, 5)), (-2, (0, 1))),
    column((7, (4, 5, 6)), (8, (5,))),
    column((7, (7,)), (8, (6, 7)), (-3, (0,))),
    column((6, (3, 4, 5, 6))),
    column((6, (7,)), (9, (6, 7)), (5, (2,))),
    column((5, (3, 4, 5, 6))),
    column((5, (7,)), (10, (7,)), (4, (1, 2))),
    column((4, (3, 4, 5, 6))),
    column((4, (7,)), (3, (0, 1, 2))),
    column((3, (3, 4, 5, 6))),
)
INC_FIRST = 10
INC_TABLE = (
    column((0, (0, 1, 2, 3))),
    column((1, (0, 1, 2, 3))),
    column((1, (4,)), (2, (0, 1, 2))),
    0,
    column((2, (3, 4, 5)), (7, (4,))),
    column((7, (5, 6, 7)), (8, (5,))),
    column((8, (6, 7)), (6, (3, 4))),
    column((6, (5, 6, 7)), (9, (6,))),
    column((9, (7,)), (-1, (0, 1, 2))),
    column((5, (2, 3, 4, 5))),
    column((5, (6, 7)), (10, (7,)), (-2, (0,))),
    column((-2, (1,)), (4, (1, 2, 3))),
    column((4, (4, 5, 6, 7))),
    column((-3, (0,)), (3, (0, 1, 2))),
    column((3, (3, 4, 5, 6))),
)


def analysis_kernel(
    anom, innov, node_h, count_h, pos_h, var_h, flags, out, xo, oi,
    held, seen, meta, node, count, pos, var, cols, xs, obs, inn, gains, total, inv, spot,
    a_s, a_r, g_s, g_r, h_s, h_r, m_s, m_r, l_s, p_s, w_s, v_s, x_s, o_s,
):
    di, j = lax.axis_index("dist"), lax.axis_index("mem")
    core = lax.rem(di, 2)
    zl, y = j // 4, lax.rem(j, 4)

    def mem_of(z, row):
        return z * 4 + lax.rem(row + 8, 4)

    def district(q):
        return q + core * (7 - 2 * q)

    small = [
        pltpu.make_async_copy(node_h, node, l_s.at[0]),
        pltpu.make_async_copy(count_h, count, l_s.at[1]),
        pltpu.make_async_copy(pos_h, pos, l_s.at[2]),
        pltpu.make_async_copy(var_h, var, l_s.at[3]),
    ]
    for copy in small:
        copy.start()

    def turn(n):
        return jnp.where(n < 3, n, 10 - n)

    def load(n):
        return pltpu.make_async_copy(anom.at[district(turn(n))], held.at[lax.rem(n, 2)], p_s.at[lax.rem(n, 2)])

    load(0).start()
    load(1).start()
    own_x = pltpu.make_async_copy(anom.at[:, pl.ds(pl.multiple_of(j * 256, 256), 256), :], xo.at[:, j], l_s.at[4])
    own_innov = pltpu.make_async_copy(innov, oi.at[1, pl.ds(3, 8), j], l_s.at[5])
    own_x.start()
    own_innov.start()

    flip = mem_of(1 - zl, y)
    other = di + 1 - 2 * core
    remote = lax.rem(di + 15 + 2 * core, 16)
    barrier = pltpu.get_barrier_semaphore()
    for k in range(1, 8):
        pl.semaphore_signal(barrier, inc=1, device_id={"dist": di, "mem": lax.rem(j + k, 8)}, device_id_type=MESH)
    pl.semaphore_signal(barrier, inc=1, device_id={"dist": other, "mem": j}, device_id_type=MESH)
    pl.semaphore_signal(barrier, inc=1, device_id={"dist": remote, "mem": flip}, device_id_type=MESH)
    pl.semaphore_wait(barrier, 9)

    def remote_copy(source, target, send, recv, dist, mem):
        return pltpu.make_async_remote_copy(
            src_ref=source, dst_ref=target, send_sem=send, recv_sem=recv,
            device_id={"dist": dist, "mem": mem}, device_id_type=MESH)

    def spread_nodes(k, q):
        d = district(q)
        target = mem_of(lax.rem(zl + k // 4, 2), y + k % 4)
        return remote_copy(
            anom.at[d, pl.ds(pl.multiple_of(target * 256, 256), 256), :], xo.at[d, j],
            a_s.at[k - 1, q], a_r.at[k - 1, q], di, target)

    def unit(u):
        early = u < 6
        kind = jnp.where(early, u // 3, lax.rem(u, 2))
        q = jnp.where(early, lax.rem(u, 3), 10 - u // 2)
        return kind, q, district(q), 1 - 2 * lax.rem(u, 2), lax.rem(u, 3) == 2

    def edge_copy(u, edge, source, block, mem):
        return remote_copy(source, block, g_s.at[edge, u], g_r.at[edge, u], di, mem)

    def forward(u, edge):
        kind, q, d, s, three = unit(u)
        here, there = zl, 1 - zl
        from_, to = {
            3: (mem_of(here, y - s), flip),
            4: (mem_of(here, y + s), jnp.where(three, flip, mem_of(here, y - s))),
            5: (jnp.where(three, mem_of(here, y - s), flip), jnp.where(three, mem_of(here, y + s), mem_of(here, y - s))),
            6: (jnp.where(three, mem_of(there, y + s), mem_of(there, y - s)),
                jnp.where(three, mem_of(here, y - s), mem_of(here, y + s))),
        }[edge]
        block = oi.at[kind, 3 + d, from_]
        return edge_copy(u, edge, block, block, to)

    def gathered(u, edge):
        kind, q, d, s, three = unit(u)
        here, there = zl, 1 - zl
        from_ = (
            mem_of(here, y - s),
            mem_of(here, y + s),
            flip,
            mem_of(there, y - s),
            jnp.where(three, mem_of(there, y + s), mem_of(here, y + 2)),
            jnp.where(three, mem_of(here, y + 2), mem_of(there, y + s)),
            mem_of(there, y + 2),
        )[edge]
        block = oi.at[kind, 3 + d, from_]
        return edge_copy(u, edge, block, block, flip)

    def halo(u):
        kind, q, d, s, three = unit(u)
        near = q >= 5
        slot = jnp.where(d >= 5, d - 5, 11 + d)
        index = jnp.where(near, q - 2, q)
        return remote_copy(
            oi.at[kind, 3 + d], oi.at[kind, slot], h_s.at[kind, index], h_r.at[kind, index],
            jnp.where(near, other, remote), jnp.where(near, j, flip))

    def halo_in(kind, index):
        slot = jnp.where(core == 0, jnp.where(index < 3, 2 - index, 16 - index), jnp.where(index < 3, 11 + index, index - 3))
        return remote_copy(oi.at[kind, slot], oi.at[kind, slot], h_s.at[kind, index], h_r.at[kind, index], other, j)

    def has_halo(u):
        q = unit(u)[1]
        return (q < 3) | (q >= 5)

    def own_seen(d):
        return pltpu.make_async_copy(seen.at[d], oi.at[0, 3 + d, j], w_s.at[d])

    for k in FAR_FIRST:
        spread_nodes(k, 0).start()
    for copy in small:
        copy.wait()
    slot8 = lax.broadcasted_iota(jnp.int32, (256, 8), 0)
    cols[...] = jnp.where(slot8 < count[...], node[...].T, -1)
    xy = pos[:, pl.ds(pl.multiple_of(j * 256, 256), 256)].astype(jnp.float32).T
    for d in range(8):
        for axis in range(2):
            spot[axis, d] = jnp.broadcast_to(xy[:, 8 * axis + d:8 * axis + d + 1], (256, 128))
        total[d] = jnp.zeros((256, 1024), jnp.float32)

    def observe(q):
        d, n = district(q), turn(q)
        load(n).wait()
        lane = lax.broadcasted_iota(jnp.int32, (256, 8), 1)
        which = jnp.sum(jnp.where(lane == d, cols[...], 0), axis=1, keepdims=True)
        hot = jnp.where(lax.broadcasted_iota(jnp.int32, (256, 2048), 1) == which, 1.0, 0.0).astype(jnp.bfloat16)
        rows = jnp.dot(hot, held[lax.rem(n, 2)], preferred_element_type=jnp.float32)
        seen[d] = rows.astype(jnp.bfloat16)
        spots = lax.dot_general(pos[...], hot, (((1,), (1,)), ((), ())), preferred_element_type=jnp.float32)
        row16 = lax.broadcasted_iota(jnp.int32, (16, 256), 0)
        row8 = lax.broadcasted_iota(jnp.int32, (8, 256), 0)
        sx = jnp.sum(jnp.where(row16 == d, spots, 0.0), axis=0, keepdims=True)
        sy = jnp.sum(jnp.where(row16 == d + 8, spots, 0.0), axis=0, keepdims=True)
        sv = jnp.sum(jnp.where(row8 == d, var[...].astype(jnp.float32), 0.0), axis=0, keepdims=True)
        meta[3 + d] = jnp.where(row8 == 0, sx, jnp.where(row8 == 1, sy, jnp.where(row8 == 2, sv, 0.0)))

        @pl.when(n < 6)
        def _():
            load(n + 2).start()

        own_seen(d).start()

    far_meta = remote_copy(
        meta.at[pl.ds(3 + 5 * core, 3)], meta.at[pl.ds(11 - 11 * core, 3)], m_s.at[0], m_r.at[0], remote, flip)
    near_meta = remote_copy(
        meta.at[pl.ds(8 - 5 * core, 3)], meta.at[pl.ds(11 * core, 3)], m_s.at[1], m_r.at[1], other, j)

    def slot_of(qe):
        return 3 + qe + core * (7 - 2 * qe)

    def bring(kind, slot, which):
        @pl.when(kind == 0)
        def _():
            pltpu.make_async_copy(oi.at[0, slot], obs.at[slot], v_s.at[which]).start()

        @pl.when(kind == 1)
        def _():
            pltpu.make_async_copy(oi.at[1, slot], inn.at[slot], v_s.at[which]).start()

    def brought(kind, slot, which):
        @pl.when(kind == 0)
        def _():
            pltpu.make_async_copy(oi.at[0, slot], obs.at[slot], v_s.at[which]).wait()
            square = jnp.zeros((256, 128), jnp.float32)
            for m in range(8):
                part = obs[slot, m].astype(jnp.float32)
                square = square + part * part
            square = jnp.sum(square.T, axis=0, keepdims=True)
            inv[pl.ds(slot, 1)] = 1.0 / (square + 1023.0 * meta[slot, 2:3])

        @pl.when(kind == 1)
        def _():
            pltpu.make_async_copy(oi.at[1, slot], inn.at[slot], v_s.at[which]).wait()

    def own_event(t, act):
        u = t - 3 * LAG

        @pl.when((u >= 0) & (u < UNITS))
        def _():
            kind, q, d, s, three = unit(u)
            act(kind, 3 + d, 0)

    def near_event(t, act, first):
        u = t - 3 * LAG - 1

        @pl.when((u >= 6) & (u < 12))
        def _():
            kind, q, d, s, three = unit(u)
            if first:
                halo_in(kind, q - 2).wait_recv()
            act(kind, slot_of(15 - q), 1)

    def far_event(t, act, first):
        early = t < 16
        i = jnp.where(early, t - 10, t - 17) // 2

        @pl.when((t == 10) | (t == 12) | (t == 14) | (t == 17) | (t == 19) | (t == 21))
        def _():
            kind = jnp.where(early, 0, 1)
            if first:
                halo_in(kind, i).wait_recv()
            act(kind, slot_of(-1 - i), 2)

    def nodes_event(t):
        for q in range(8):
            @pl.when(t == X_STEP[q])
            def _():
                d = district(q)
                if q == 0:
                    own_x.wait()
                for k in range(1, 8):
                    source = mem_of(lax.rem(zl + k // 4, 2), y + 4 - k % 4)
                    block = xo.at[d, source]
                    remote_copy(block, block, a_s.at[k - 1, q], a_r.at[k - 1, q], di, flip).wait_recv()
                pltpu.make_async_copy(xo.at[d], xs.at[d], x_s).start()

            @pl.when(t == X_STEP[q] + 1)
            def _():
                pltpu.make_async_copy(xo.at[district(q)], xs.at[district(q)], x_s).wait()

    def tasks(t, table, first):
        code = jnp.int32(0)
        for i, word in enumerate(table):
            if word:
                code = jnp.where(t == first + i, word, code)
        return code

    def places(code, i):
        item = lax.rem(code // (128 ** i), 128)
        d, slot = district(lax.rem(item, 8)), slot_of(item // 8 - 3)
        return d, slot, slot - d

    def joined(ref, index):
        return jnp.concatenate([ref[index, m] for m in range(8)], axis=1)

    def gain_block(t):
        code = tasks(t, GAIN_TABLE, GAIN_FIRST)

        @pl.when((t >= GAIN_FIRST) & (t < GAIN_FIRST + len(GAIN_TABLE)))
        def _():
            for i in range(4):
                d, slot, s = places(code, i)
                cov = lax.dot_general(joined(xs, d), joined(obs, slot), (((1,), (1,)), ((), ())), preferred_element_type=jnp.float32)
                row = inv[pl.ds(slot, 1)] * flags[d, s].astype(jnp.float32)
                node_x, node_y = spot[0, d], spot[1, d]
                weight = taper(
                    jnp.concatenate([node_x, node_x], axis=1), jnp.concatenate([node_y, node_y], axis=1),
                    meta[slot], (s - RADIUS).astype(jnp.float32))
                gains[d, s] = (weight * cov * row).astype(jnp.bfloat16)

    def increment_block(t):
        code = tasks(t, INC_TABLE, INC_FIRST)

        @pl.when(code > 0)
        def _():
            for i in range(4):
                d, slot, s = places(code, i)
                total[d] += jnp.dot(gains[d, s], joined(inn, slot), preferred_element_type=jnp.float32)

    def finish(q):
        d = district(q)
        return pltpu.make_async_copy(total.at[d], out.at[d], o_s.at[q])

    def step(t, carry):
        @pl.when(t < UNITS)
        def _():
            kind, q, d, s, three = unit(t)
            targets = (mem_of(zl, y + s), mem_of(zl, y - s), flip)

            @pl.when(kind == 0)
            def _():
                observe(q)
                for edge in range(3):
                    edge_copy(t, edge, seen.at[d], oi.at[0, 3 + d, j], targets[edge]).start()

            @pl.when(kind == 1)
            def _():
                for edge in range(3):
                    edge_copy(t, edge, innov.at[d], oi.at[1, 3 + d, j], targets[edge]).start()

        @pl.when((t >= 1) & (t < 11) & (lax.rem(t, 3) < 2))
        def _():
            for k in FAR_FIRST:
                spread_nodes(k, t - t // 3).start()

        @pl.when(t == 3)
        def _():
            far_meta.start()

        @pl.when(t == 9)
        def _():
            far_meta.wait_recv()

        @pl.when(t == 11)
        def _():
            near_meta.start()

        @pl.when(t == 13)
        def _():
            near_meta.wait_recv()

        own_event(t - 1, brought)
        near_event(t - 1, brought, False)
        far_event(t - 1, brought, False)

        u = t - LAG

        @pl.when((u >= 0) & (u < UNITS))
        def _():
            for edge in range(3):
                gathered(u, edge).wait_recv()
                forward(u, edge + 3).start()

        v = t - 2 * LAG

        @pl.when((v >= 0) & (v < UNITS))
        def _():
            gathered_last(v, True)
            forward(v, 6).start()

        w = t - 3 * LAG

        @pl.when((w >= 0) & (w < UNITS))
        def _():
            gathered_last(w, False)
            gathered(w, 5).wait_recv()
            gathered(w, 6).wait_recv()
            kind, q, d, s, three = unit(w)

            @pl.when(kind == 0)
            def _():
                own_seen(d).wait()

            @pl.when(w == 3)
            def _():
                own_innov.wait()

            @pl.when(has_halo(w))
            def _():
                halo(w).start()

        own_event(t, bring)
        near_event(t, bring, True)
        far_event(t, bring, True)
        nodes_event(t)
        gain_block(t)
        increment_block(t)

        @pl.when(t == STEPS - 2)
        def _():
            for q in (0, 1, 2, 7):
                finish(q).start()

        return carry

    def gathered_last(u, first):
        three = unit(u)[4]
        take4 = three if first else jnp.logical_not(three)

        @pl.when(take4)
        def _():
            gathered(u, 4).wait_recv()

        @pl.when(jnp.logical_not(take4))
        def _():
            gathered(u, 3).wait_recv()

    lax.fori_loop(0, STEPS, step, 0)
    for q in (3, 4, 5, 6):
        finish(q).start()

    def drain(u, carry):
        for edge in range(7):
            gathered(u, edge).wait_send()

        @pl.when(has_halo(u))
        def _():
            halo(u).wait_send()

        return carry

    lax.fori_loop(0, UNITS, drain, 0)

    def drain_nodes(q, carry):
        for k in range(1, 8):
            spread_nodes(k, q).wait_send()
        return carry

    lax.fori_loop(0, 8, drain_nodes, 0)
    far_meta.wait_send()
    near_meta.wait_send()
    for q in range(8):
        finish(q).wait()


def taper(node_x, node_y, meta, shift):
    dx = (meta[0:1] + shift) - node_x
    dy = meta[1:2] - node_y
    square = jnp.maximum((dx * dx + dy * dy) * (1.0 / (REACH * REACH)), 1e-30)
    root = lax.rsqrt(square)
    z = square * root
    inner = (((-0.25 * z + 0.5) * z + 0.625) * z - 5.0 / 3.0) * square + 1.0
    left = jnp.maximum(2.0 - z, 0.0)
    left = left * left
    outer = (left * left) * (z * (1.0 / 12.0) + (1.0 / 6.0) - root * (1.0 / 24.0))
    return jnp.where(z < 1.0, inner, outer)


def analysis(anomalies, innovations, obs_var, node_pos, obs_node, obs_count, in_radius):
    bf16, f32 = jnp.bfloat16, jnp.float32
    return pl.pallas_call(
        analysis_kernel,
        out_shape=(
            jax.ShapeDtypeStruct((8, 256, 1024), f32),
            jax.ShapeDtypeStruct((8, 8, 256, 128), bf16),
            jax.ShapeDtypeStruct((2, 14, 8, 256, 128), bf16),
        ),
        in_specs=[HBM] * 6 + [SMEM],
        out_specs=(HBM,) * 3,
        scratch_shapes=[
            pltpu.VMEM((2, 2048, 128), bf16),
            pltpu.VMEM((8, 256, 128), bf16),
            pltpu.VMEM((14, 8, 256), f32),
            pltpu.VMEM((8, 256), jnp.int32),
            pltpu.VMEM((1, 8), jnp.int32),
            pltpu.VMEM((16, 2048), bf16),
            pltpu.VMEM((8, 256), bf16),
            pltpu.VMEM((256, 8), jnp.int32),
            pltpu.VMEM((8, 8, 256, 128), bf16),
            pltpu.VMEM((14, 8, 256, 128), bf16),
            pltpu.VMEM((14, 8, 256, 128), bf16),
            pltpu.VMEM((8, 7, 256, 256), bf16),
            pltpu.VMEM((8, 256, 1024), f32),
            pltpu.VMEM((14, 256), f32),
            pltpu.VMEM((2, 8, 256, 128), f32),
            DMA((7, 8)), DMA((7, 8)), DMA((7, UNITS)), DMA((7, UNITS)), DMA((2, 6)), DMA((2, 6)), DMA((2,)), DMA((2,)),
            DMA((6,)), DMA((2,)), DMA((8,)), DMA((3,)), DMA, DMA((8,)),
        ],
        compiler_params=pltpu.CompilerParams(collective_id=0, has_side_effects=True, vmem_limit_bytes=58 << 20),
    )(anomalies, innovations, obs_node, obs_count.reshape(1, 8), node_pos.reshape(16, 2048), obs_var, in_radius)[0]


def on_device(*arrays):
    return analysis(*arrays)


def solution(mesh):
    return jax.shard_map(
        on_device,
        mesh=mesh,
        in_specs=(
            P("dist", None, "mem"),
            P("dist", None, "mem"),
            P("dist", None),
            P(None, "dist", None),
            P("dist", None),
            P("dist"),
            P("dist", None),
        ),
        out_specs=P("dist", "mem", None),
        check_vma=False,
    )
```

```python
import jax
import jax.numpy as jnp
from jax import lax
from jax.experimental import pallas as pl
from jax.experimental.pallas import tpu as pltpu
from jax.sharding import PartitionSpec as P

MESH = pl.DeviceIdType.MESH
HBM = pl.BlockSpec(memory_space=pltpu.HBM)
VMEM = pl.BlockSpec(memory_space=pltpu.VMEM)
SMEM = pl.BlockSpec(memory_space=pltpu.SMEM)
DMA = pltpu.SemaphoreType.DMA
RADIUS = 3
REACH = 2.5
UNITS = 16
LAG = 2
FAR_FIRST = (6, 2, 5, 7, 4, 1, 3)
STEPS = 22
OWN_USED = 14
NODE_TURN = (1, 0, 2, 3, 4, 5, 6, 7)


def column(*pairs):
    return sum(((e + 3) * 8 + d) * 128 ** i for i, (e, d) in enumerate(pairs))


GAIN_FIRST = 8
GAIN_TABLE = (
    column((0, 0), (0, 1), (1, 0), (1, 1)),
    column((0, 2), (1, 2), (2, 0), (2, 1)),
    column((2, 2), (3, 0), (3, 1), (3, 2)),
    column((0, 3), (1, 3), (-1, 0), (-1, 1)),
    column((-1, 2), (2, 3), (4, 1), (4, 2)),
    column((1, 4), (2, 4), (-2, 0), (-2, 1)),
    column((5, 2), (5, 3), (5, 4), (4, 3)),
    column((2, 5), (6, 3), (6, 4), (6, 5)),
    column((-3, 0), (5, 5), (4, 4), (4, 5)),
    column((7, 4), (7, 5), (7, 6), (6, 6)),
    column((8, 5), (8, 6), (5, 6), (9, 6)),
    column((7, 7), (6, 7), (8, 7), (5, 7)),
    column((9, 7), (4, 6), (4, 7), (10, 7)),
    column((3, 3), (3, 4), (3, 5), (3, 6)),
)
INC_FIRST = 12
INC_TABLE = (
    column((0, 0), (0, 1), (0, 2), (0, 3)),
    0,
    column((1, 0), (1, 1), (1, 2), (1, 3)),
    0,
    column((1, 4), (2, 0), (2, 1), (2, 2)),
    column((-1, 0), (-1, 1), (-1, 2), (2, 3)),
    column((2, 4), (2, 5), (-2, 0), (-2, 1)),
    column((7, 4), (7, 5), (7, 6), (7, 7)),
    column((6, 3), (6, 4), (6, 5), (6, 6)),
    column((8, 5), (8, 6), (6, 7), (8, 7)),
)
LATE = (
    (-3, 3,),
    (3, 4,),
    (3, 4, 5,),
    (3, 4, 5,),
    (3, 4, 5,),
    (3, 4, 5,),
    (3, 4, 5, 9,),
    (4, 5, 9, 10,),
)


MOST = max(len(others) for others in LATE)


def analysis_kernel(
    anom, innov, node_h, count_h, pos_h, var_h, flags, out, late, xo, oi,
    held, seen, meta, node, count, pos, var, cols, xs, obs, inn, gains, total, inv, spot,
    a_s, a_r, g_s, g_r, h_s, h_r, m_s, m_r, l_s, p_s, w_s, v_s, x_s, o_s, f_s,
):
    di, j = lax.axis_index("dist"), lax.axis_index("mem")
    core = lax.rem(di, 2)
    zl, y = j // 4, lax.rem(j, 4)

    def mem_of(z, row):
        return z * 4 + lax.rem(row + 8, 4)

    def district(q):
        return q + core * (7 - 2 * q)

    small = [
        pltpu.make_async_copy(node_h, node, l_s.at[0]),
        pltpu.make_async_copy(count_h, count, l_s.at[1]),
        pltpu.make_async_copy(pos_h, pos, l_s.at[2]),
        pltpu.make_async_copy(var_h, var, l_s.at[3]),
    ]
    for copy in small:
        copy.start()

    def load(n):
        return pltpu.make_async_copy(anom.at[district(n)], held.at[lax.rem(n, 2)], p_s.at[lax.rem(n, 2)])

    load(0).start()
    load(1).start()
    own_x = pltpu.make_async_copy(anom.at[:, pl.ds(pl.multiple_of(j * 256, 256), 256), :], xo.at[:, j], l_s.at[4])
    own_innov = pltpu.make_async_copy(innov, oi.at[1, pl.ds(3, 8), j], l_s.at[5])
    own_x.start()
    own_innov.start()

    flip = mem_of(1 - zl, y)
    other = di + 1 - 2 * core
    remote = lax.rem(di + 15 + 2 * core, 16)
    barrier = pltpu.get_barrier_semaphore()
    for k in range(1, 8):
        pl.semaphore_signal(barrier, inc=1, device_id={"dist": di, "mem": lax.rem(j + k, 8)}, device_id_type=MESH)
    pl.semaphore_signal(barrier, inc=1, device_id={"dist": other, "mem": j}, device_id_type=MESH)
    pl.semaphore_signal(barrier, inc=1, device_id={"dist": remote, "mem": flip}, device_id_type=MESH)
    for d in range(8):
        total[d] = jnp.zeros((256, 1024), jnp.float32)
    pl.semaphore_wait(barrier, 9)

    def remote_copy(source, target, send, recv, dist, mem):
        return pltpu.make_async_remote_copy(
            src_ref=source, dst_ref=target, send_sem=send, recv_sem=recv,
            device_id={"dist": dist, "mem": mem}, device_id_type=MESH)

    def spread_nodes(k, q):
        d = district(q)
        target = mem_of(lax.rem(zl + k // 4, 2), y + k % 4)
        return remote_copy(
            anom.at[d, pl.ds(pl.multiple_of(target * 256, 256), 256), :], xo.at[d, j],
            a_s.at[k - 1, q], a_r.at[k - 1, q], di, target)

    def unit(u):
        middle = (u >= 5) & (u < 11)
        odd = lax.rem(u, 2)
        kind = jnp.where(middle, odd, jnp.where(u < 5, 0, 1))
        q = jnp.where(middle, jnp.where(odd == 1, (u - 5) // 2, 2 + u // 2), jnp.where(u < 5, u, 18 - u))
        return kind, q, district(q), 1 - 2 * lax.rem(u, 2), lax.rem(u, 3) == 2

    def edge_copy(u, edge, source, block, mem):
        return remote_copy(source, block, g_s.at[edge, u], g_r.at[edge, u], di, mem)

    def forward(u, edge):
        kind, q, d, s, three = unit(u)
        here, there = zl, 1 - zl
        from_, to = {
            3: (mem_of(here, y - s), flip),
            4: (mem_of(here, y + s), jnp.where(three, flip, mem_of(here, y - s))),
            5: (jnp.where(three, mem_of(here, y - s), flip), jnp.where(three, mem_of(here, y + s), mem_of(here, y - s))),
            6: (jnp.where(three, mem_of(there, y + s), mem_of(there, y - s)),
                jnp.where(three, mem_of(here, y - s), mem_of(here, y + s))),
        }[edge]
        block = oi.at[kind, 3 + d, from_]
        return edge_copy(u, edge, block, block, to)

    def gathered(u, edge):
        kind, q, d, s, three = unit(u)
        here, there = zl, 1 - zl
        from_ = (
            mem_of(here, y - s),
            mem_of(here, y + s),
            flip,
            mem_of(there, y - s),
            jnp.where(three, mem_of(there, y + s), mem_of(here, y + 2)),
            jnp.where(three, mem_of(here, y + 2), mem_of(there, y + s)),
            mem_of(there, y + 2),
        )[edge]
        block = oi.at[kind, 3 + d, from_]
        return edge_copy(u, edge, block, block, flip)

    def halo(u):
        kind, q, d, s, three = unit(u)
        near = q >= 5
        slot = jnp.where(d >= 5, d - 5, 11 + d)
        index = jnp.where(near, q - 2, q)
        return remote_copy(
            oi.at[kind, 3 + d], oi.at[kind, slot], h_s.at[kind, index], h_r.at[kind, index],
            jnp.where(near, other, remote), jnp.where(near, j, flip))

    def halo_in(kind, index):
        slot = jnp.where(core == 0, jnp.where(index < 3, 2 - index, 16 - index), jnp.where(index < 3, 11 + index, index - 3))
        return remote_copy(oi.at[kind, slot], oi.at[kind, slot], h_s.at[kind, index], h_r.at[kind, index], other, j)

    def has_halo(u):
        q = unit(u)[1]
        return (q < 3) | (q >= 5)

    def own_seen(d):
        return pltpu.make_async_copy(seen.at[d], oi.at[0, 3 + d, j], w_s.at[d])

    for k in FAR_FIRST[:3]:
        spread_nodes(k, NODE_TURN[0]).start()
    for copy in small:
        copy.wait()
    slot8 = lax.broadcasted_iota(jnp.int32, (256, 8), 0)
    cols[...] = jnp.where(slot8 < count[...], node[...].T, -1)
    xy = pos[:, pl.ds(pl.multiple_of(j * 256, 256), 256)].astype(jnp.float32).T
    for d in range(8):
        for axis in range(2):
            spot[axis, d] = jnp.broadcast_to(xy[:, 8 * axis + d:8 * axis + d + 1], (256, 128))

    def observe(q):
        d, n = district(q), q
        load(n).wait()
        lane = lax.broadcasted_iota(jnp.int32, (256, 8), 1)
        which = jnp.sum(jnp.where(lane == d, cols[...], 0), axis=1, keepdims=True)
        hot = jnp.where(lax.broadcasted_iota(jnp.int32, (256, 2048), 1) == which, 1.0, 0.0).astype(jnp.bfloat16)
        rows = jnp.dot(hot, held[lax.rem(n, 2)], preferred_element_type=jnp.float32)
        seen[d] = rows.astype(jnp.bfloat16)
        spots = lax.dot_general(pos[...], hot, (((1,), (1,)), ((), ())), preferred_element_type=jnp.float32)
        row16 = lax.broadcasted_iota(jnp.int32, (16, 256), 0)
        row8 = lax.broadcasted_iota(jnp.int32, (8, 256), 0)
        sx = jnp.sum(jnp.where(row16 == d, spots, 0.0), axis=0, keepdims=True)
        sy = jnp.sum(jnp.where(row16 == d + 8, spots, 0.0), axis=0, keepdims=True)
        sv = jnp.sum(jnp.where(row8 == d, var[...].astype(jnp.float32), 0.0), axis=0, keepdims=True)
        meta[3 + d] = jnp.where(row8 == 0, sx, jnp.where(row8 == 1, sy, jnp.where(row8 == 2, sv, 0.0)))

        @pl.when(n < 6)
        def _():
            load(n + 2).start()

        own_seen(d).start()

    far_meta = remote_copy(
        meta.at[pl.ds(3 + 5 * core, 3)], meta.at[pl.ds(11 - 11 * core, 3)], m_s.at[0], m_r.at[0], remote, flip)
    near_meta = remote_copy(
        meta.at[pl.ds(8 - 5 * core, 3)], meta.at[pl.ds(11 * core, 3)], m_s.at[1], m_r.at[1], other, j)

    def slot_of(qe):
        return 3 + qe + core * (7 - 2 * qe)

    def bring(kind, slot, which):
        @pl.when(kind == 0)
        def _():
            pltpu.make_async_copy(oi.at[0, slot], obs.at[slot], v_s.at[which]).start()

        @pl.when(kind == 1)
        def _():
            pltpu.make_async_copy(oi.at[1, slot], inn.at[slot], v_s.at[which]).start()

    def brought(kind, slot, which):
        @pl.when(kind == 0)
        def _():
            pltpu.make_async_copy(oi.at[0, slot], obs.at[slot], v_s.at[which]).wait()
            square = jnp.zeros((256, 128), jnp.float32)
            for m in range(8):
                part = obs[slot, m].astype(jnp.float32)
                square = square + part * part
            square = jnp.sum(square.T, axis=0, keepdims=True)
            inv[pl.ds(slot, 1)] = 1.0 / (square + 1023.0 * meta[slot, 2:3])

        @pl.when(kind == 1)
        def _():
            pltpu.make_async_copy(oi.at[1, slot], inn.at[slot], v_s.at[which]).wait()

    def own_event(t, act):
        u = t - 3 * LAG

        @pl.when((u >= 0) & (u < OWN_USED))
        def _():
            kind, q, d, s, three = unit(u)
            act(kind, 3 + d, 0)

    def near_event(t, act, first):
        u = t - 3 * LAG - 1

        @pl.when((u == 6) | (u == 8) | ((u >= 10) & (u < 14)))
        def _():
            kind, q, d, s, three = unit(u)
            if first:
                halo_in(kind, q - 2).wait_recv()
            act(kind, slot_of(15 - q), 1)

    def far_event(t, act, first):
        early = t < 15
        i = jnp.where(early, t - 10, t - 15) // 2

        @pl.when((t == 10) | (t == 12) | (t == 14) | (t == 15) | (t == 17) | (t == 19))
        def _():
            kind = jnp.where(early, 0, 1)
            if first:
                halo_in(kind, i).wait_recv()
            act(kind, slot_of(-1 - i), 2)

    def nodes_copy(q):
        return pltpu.make_async_copy(xo.at[district(q)], xs.at[district(q)], x_s)

    def nodes_event(t):
        turn = t // 2 - 2
        q = jnp.where(turn < 2, 1 - turn, turn)

        @pl.when(t == 4)
        def _():
            own_x.wait()

        @pl.when((turn >= 0) & (turn < 8) & (lax.rem(t, 2) == 0))
        def _():
            d = district(q)
            for k in range(1, 8):
                source = mem_of(lax.rem(zl + k // 4, 2), y + 4 - k % 4)
                block = xo.at[d, source]
                remote_copy(block, block, a_s.at[k - 1, q], a_r.at[k - 1, q], di, flip).wait_recv()
            nodes_copy(q).start()

        @pl.when((turn >= 0) & (turn < 8) & (lax.rem(t, 2) == 1))
        def _():
            nodes_copy(q).wait()

    def tasks(t, table, first):
        code = jnp.int32(0)
        for i, word in enumerate(table):
            if word:
                code = jnp.where(t == first + i, word, code)
        return code

    def places(code, i):
        item = lax.rem(code // (128 ** i), 128)
        d, slot = district(lax.rem(item, 8)), slot_of(item // 8 - 3)
        return d, slot, slot - d

    def joined(ref, index):
        return jnp.concatenate([ref[index, m] for m in range(8)], axis=1)

    def gain_block(t, part):
        code = tasks(t, GAIN_TABLE, GAIN_FIRST)

        @pl.when((t >= GAIN_FIRST) & (t < GAIN_FIRST + len(GAIN_TABLE)))
        def _():
            for i in part:
                d, slot, s = places(code, i)
                cov = lax.dot_general(joined(xs, d), joined(obs, slot), (((1,), (1,)), ((), ())), preferred_element_type=jnp.float32)
                row = inv[pl.ds(slot, 1)] * flags[d, s].astype(jnp.float32)
                node_x, node_y = spot[0, d], spot[1, d]
                weight = taper(
                    jnp.concatenate([node_x, node_x], axis=1), jnp.concatenate([node_y, node_y], axis=1),
                    meta[slot], (s - RADIUS).astype(jnp.float32))
                gains[d, s] = (weight * cov * row).astype(jnp.bfloat16)

    def increment_block(t):
        code = tasks(t, INC_TABLE, INC_FIRST)

        @pl.when(code > 0)
        def _():
            for i in range(4):
                d, slot, s = places(code, i)
                total[d] += jnp.dot(gains[d, s], joined(inn, slot), preferred_element_type=jnp.float32)

    def hand_over():
        copies = []
        for q, others in enumerate(LATE):
            for r, e in enumerate(others):
                d = district(q)
                copies.append(pltpu.make_async_copy(gains.at[d, slot_of(e) - d], late.at[d, r], f_s.at[q, r]))
        return copies

    def finish(q):
        d = district(q)
        return pltpu.make_async_copy(total.at[d], out.at[d], o_s.at[q])

    def step(t, carry):
        @pl.when(t < UNITS)
        def _():
            kind, q, d, s, three = unit(t)
            targets = (mem_of(zl, y + s), mem_of(zl, y - s), flip)

            @pl.when(kind == 0)
            def _():
                observe(q)
                for edge in range(3):
                    edge_copy(t, edge, seen.at[d], oi.at[0, 3 + d, j], targets[edge]).start()

            @pl.when(kind == 1)
            def _():
                for edge in range(3):
                    edge_copy(t, edge, innov.at[d], oi.at[1, 3 + d, j], targets[edge]).start()

        turn = t // 2
        place = jnp.where(turn < 2, 1 - turn, turn)

        @pl.when((t >= 1) & (t < 16) & (lax.rem(t, 2) == 0))
        def _():
            for k in FAR_FIRST[:3]:
                spread_nodes(k, place).start()

        @pl.when((t < 16) & (lax.rem(t, 2) == 1))
        def _():
            for k in FAR_FIRST[3:]:
                spread_nodes(k, place).start()

        @pl.when(t == 3)
        def _():
            far_meta.start()

        @pl.when(t == 9)
        def _():
            far_meta.wait_recv()

        @pl.when(t == 11)
        def _():
            near_meta.start()

        @pl.when(t == 13)
        def _():
            near_meta.wait_recv()

        own_event(t - 1, brought)
        near_event(t - 1, brought, False)
        far_event(t - 1, brought, False)

        u = t - LAG

        @pl.when((u >= 0) & (u < UNITS))
        def _():
            for edge in range(3):
                gathered(u, edge).wait_recv()
                forward(u, edge + 3).start()

        nodes_event(t)
        gain_block(t, (0, 1))

        v = t - 2 * LAG

        @pl.when((v >= 0) & (v < UNITS))
        def _():
            gathered_last(v, True)
            forward(v, 6).start()

        gain_block(t, (2, 3))
        increment_block(t)

        @pl.when(t == STEPS - 1)
        def _():
            for copy in hand_over():
                copy.start()
            for q in range(8):
                finish(q).start()

        w = t - 3 * LAG

        @pl.when((w >= 0) & (w < UNITS))
        def _():
            gathered_last(w, False)
            gathered(w, 5).wait_recv()
            gathered(w, 6).wait_recv()
            kind, q, d, s, three = unit(w)

            @pl.when(kind == 0)
            def _():
                own_seen(d).wait()

            @pl.when(w == 3)
            def _():
                own_innov.wait()

            @pl.when(has_halo(w))
            def _():
                halo(w).start()

        own_event(t, bring)
        near_event(t, bring, True)
        far_event(t, bring, True)
        return carry

    def gathered_last(u, first):
        three = unit(u)[4]
        take4 = three if first else jnp.logical_not(three)

        @pl.when(take4)
        def _():
            gathered(u, 4).wait_recv()

        @pl.when(jnp.logical_not(take4))
        def _():
            gathered(u, 3).wait_recv()

    lax.fori_loop(0, STEPS, step, 0)
    near_event(jnp.int32(STEPS - 1), brought, False)

    def drain(u, carry):
        for edge in range(7):
            gathered(u, edge).wait_send()

        @pl.when(has_halo(u))
        def _():
            halo(u).wait_send()

        return carry

    lax.fori_loop(0, UNITS, drain, 0)

    def drain_nodes(q, carry):
        for k in range(1, 8):
            spread_nodes(k, q).wait_send()
        return carry

    lax.fori_loop(0, 8, drain_nodes, 0)
    far_meta.wait_send()
    near_meta.wait_send()
    for q in range(8):
        finish(q).wait()
    for copy in hand_over():
        copy.wait()


def taper(node_x, node_y, meta, shift):
    dx = (meta[0:1] + shift) - node_x
    dy = meta[1:2] - node_y
    square = jnp.maximum((dx * dx + dy * dy) * (1.0 / (REACH * REACH)), 1e-30)
    root = lax.rsqrt(square)
    z = square * root
    inner = (((-0.25 * z + 0.5) * z + 0.625) * z - 5.0 / 3.0) * square + 1.0
    left = jnp.maximum(2.0 - z, 0.0)
    left = left * left
    outer = (left * left) * (z * (1.0 / 12.0) + (1.0 / 6.0) - root * (1.0 / 24.0))
    return jnp.where(z < 1.0, inner, outer)


def analysis(anomalies, innovations, obs_var, node_pos, obs_node, obs_count, in_radius):
    bf16, f32 = jnp.bfloat16, jnp.float32
    return pl.pallas_call(
        analysis_kernel,
        out_shape=(
            jax.ShapeDtypeStruct((8, 256, 1024), f32),
            jax.ShapeDtypeStruct((8, MOST, 256, 256), bf16),
            jax.ShapeDtypeStruct((8, 8, 256, 128), bf16),
            jax.ShapeDtypeStruct((2, 14, 8, 256, 128), bf16),
        ),
        in_specs=[HBM] * 6 + [SMEM],
        out_specs=(HBM,) * 4,
        scratch_shapes=[
            pltpu.VMEM((2, 2048, 128), bf16),
            pltpu.VMEM((8, 256, 128), bf16),
            pltpu.VMEM((14, 8, 256), f32),
            pltpu.VMEM((8, 256), jnp.int32),
            pltpu.VMEM((1, 8), jnp.int32),
            pltpu.VMEM((16, 2048), bf16),
            pltpu.VMEM((8, 256), bf16),
            pltpu.VMEM((256, 8), jnp.int32),
            pltpu.VMEM((8, 8, 256, 128), bf16),
            pltpu.VMEM((14, 8, 256, 128), bf16),
            pltpu.VMEM((14, 8, 256, 128), bf16),
            pltpu.VMEM((8, 7, 256, 256), bf16),
            pltpu.VMEM((8, 256, 1024), f32),
            pltpu.VMEM((14, 256), f32),
            pltpu.VMEM((2, 8, 256, 128), f32),
            DMA((7, 8)), DMA((7, 8)), DMA((7, UNITS)), DMA((7, UNITS)), DMA((2, 6)), DMA((2, 6)), DMA((2,)), DMA((2,)),
            DMA((6,)), DMA((2,)), DMA((8,)), DMA((3,)), DMA, DMA((8,)), DMA((8, MOST)),
        ],
        compiler_params=pltpu.CompilerParams(collective_id=0, has_side_effects=True, vmem_limit_bytes=58 << 20),
    )(anomalies, innovations, obs_node, obs_count.reshape(1, 8), node_pos.reshape(16, 2048), obs_var, in_radius)


def closing_kernel(flags, total, late_h, oi, out, gains, inn, i_s, g_s):
    d = pl.program_id(0)
    core = lax.rem(lax.axis_index("dist"), 2)

    def slot_of(qe):
        return 3 + qe + core * (7 - 2 * qe)

    used = sorted({e for others in LATE for e in others})
    innovations = [
        pltpu.make_async_copy(oi.at[1, slot_of(e)], inn.at[slot_of(e)], i_s.at[i]) for i, e in enumerate(used)]
    gains_in = pltpu.make_async_copy(late_h, gains, g_s)

    @pl.when(d == 0)
    def _():
        gains_in.start()
        for copy in innovations:
            copy.start()

    out[0] = total[0]

    @pl.when(d == 0)
    def _():
        gains_in.wait()
        for copy in innovations:
            copy.wait()

    q = d + core * (7 - 2 * d)
    code = jnp.int32(0)
    for place, others in enumerate(LATE):
        code = jnp.where(q == place, sum((e + 4) * 16 ** r for r, e in enumerate(others)), code)

    def add(r, code):
        item = lax.rem(code, 16)
        slot = slot_of(item - 4)
        s = jnp.clip(slot - d, 0, 6)

        @pl.when((item > 0) & (flags[d, s] > 0))
        def _():
            rows = jnp.concatenate([inn[slot, m] for m in range(8)], axis=1)
            out[0] += jnp.dot(gains[d, r], rows, preferred_element_type=jnp.float32)

        return code // 16

    lax.fori_loop(0, MOST, add, code)


def closing(in_radius, total, late, oi):
    used = len({e for others in LATE for e in others})
    block = pl.BlockSpec((1, 256, 1024), lambda d: (d, 0, 0))
    return pl.pallas_call(
        closing_kernel,
        grid=(8,),
        out_shape=jax.ShapeDtypeStruct((8, 256, 1024), jnp.float32),
        in_specs=[SMEM, block, HBM, HBM],
        out_specs=block,
        scratch_shapes=[
            pltpu.VMEM((8, MOST, 256, 256), jnp.bfloat16),
            pltpu.VMEM((14, 8, 256, 128), jnp.bfloat16),
            DMA((used,)),
            DMA,
        ],
        compiler_params=pltpu.CompilerParams(vmem_limit_bytes=56 << 20),
    )(in_radius, total, late, oi)


def on_device(*arrays):
    total, late, xo, oi = analysis(*arrays)
    return closing(arrays[-1], total, late, oi)


def solution(mesh):
    return jax.shard_map(
        on_device,
        mesh=mesh,
        in_specs=(
            P("dist", None, "mem"),
            P("dist", None, "mem"),
            P("dist", None),
            P(None, "dist", None),
            P("dist", None),
            P("dist"),
            P("dist", None),
        ),
        out_specs=P("dist", "mem", None),
        check_vma=False,
    )
```

```python
import jax
import jax.numpy as jnp
from jax import lax
from jax.experimental import pallas as pl
from jax.experimental.pallas import tpu as pltpu
from jax.sharding import PartitionSpec as P

MESH = pl.DeviceIdType.MESH
HBM = pl.BlockSpec(memory_space=pltpu.HBM)
VMEM = pl.BlockSpec(memory_space=pltpu.VMEM)
SMEM = pl.BlockSpec(memory_space=pltpu.SMEM)
DMA = pltpu.SemaphoreType.DMA
RADIUS = 3
REACH = 2.5
UNITS = 16
LAG = 2
FAR_FIRST = (6, 2, 5, 7, 4, 1, 3)
STEPS = 22
OWN_USED = 14
NODE_TURN = (1, 0, 2, 3, 4, 5, 6, 7)


def column(*pairs):
    return sum(((e + 3) * 8 + d) * 128 ** i for i, (e, d) in enumerate(pairs))


GAIN_FIRST = 8
GAIN_TABLE = (
    column((0, 0), (0, 1), (1, 0), (1, 1)),
    column((0, 2), (1, 2), (2, 0), (2, 1)),
    column((2, 2), (3, 0), (3, 1), (3, 2)),
    column((0, 3), (1, 3), (-1, 0), (-1, 1)),
    column((-1, 2), (2, 3), (4, 1), (4, 2)),
    column((1, 4), (2, 4), (-2, 0), (-2, 1)),
    column((5, 2), (5, 3), (5, 4), (4, 3)),
    column((2, 5), (6, 3), (6, 4), (6, 5)),
    column((-3, 0), (5, 5), (4, 4), (4, 5)),
    column((7, 4), (7, 5), (7, 6), (6, 6)),
    column((8, 5), (8, 6), (5, 6), (9, 6)),
    column((7, 7), (6, 7), (8, 7), (5, 7)),
    column((9, 7), (4, 6), (4, 7), (10, 7)),
    column((3, 3), (3, 4), (3, 5), (3, 6)),
)
INC_FIRST = 12
INC_TABLE = (
    column((0, 0), (0, 1), (0, 2), (0, 3)),
    0,
    column((1, 0), (1, 1), (1, 2), (1, 3)),
    0,
    column((1, 4), (2, 0), (2, 1), (2, 2)),
    column((-1, 0), (-1, 1), (-1, 2), (2, 3)),
    column((2, 4), (2, 5), (-2, 0), (-2, 1)),
    column((7, 4), (7, 5), (7, 6), (7, 7)),
    column((6, 3), (6, 4), (6, 5), (6, 6)),
)
LATE = (
    (-3, 3,),
    (3, 4,),
    (3, 4, 5,),
    (3, 4, 5,),
    (3, 4, 5,),
    (3, 4, 5, 8,),
    (3, 4, 5, 8, 9,),
    (4, 5, 6, 8, 9, 10,),
)


LAST_GAINS = ((3, 3), (3, 4), (3, 5), (3, 6))
MOST = max(len(others) for others in LATE)


def analysis_kernel(
    anom, innov, node_h, count_h, pos_h, var_h, flags, out, late, xo, oi,
    held, seen, meta, node, count, pos, var, cols, xs, obs, inn, gains, total, inv, spot,
    a_s, a_r, g_s, g_r, h_s, h_r, m_s, m_r, l_s, p_s, w_s, v_s, x_s, o_s, f_s,
):
    di, j = lax.axis_index("dist"), lax.axis_index("mem")
    core = lax.rem(di, 2)
    zl, y = j // 4, lax.rem(j, 4)

    def mem_of(z, row):
        return z * 4 + lax.rem(row + 8, 4)

    def district(q):
        return q + core * (7 - 2 * q)

    small = [
        pltpu.make_async_copy(node_h, node, l_s.at[0]),
        pltpu.make_async_copy(count_h, count, l_s.at[1]),
        pltpu.make_async_copy(pos_h, pos, l_s.at[2]),
        pltpu.make_async_copy(var_h, var, l_s.at[3]),
    ]
    for copy in small:
        copy.start()

    def load(n):
        return pltpu.make_async_copy(anom.at[district(n)], held.at[lax.rem(n, 2)], p_s.at[lax.rem(n, 2)])

    load(0).start()
    load(1).start()
    own_x = pltpu.make_async_copy(anom.at[:, pl.ds(pl.multiple_of(j * 256, 256), 256), :], xo.at[:, j], l_s.at[4])
    own_innov = pltpu.make_async_copy(innov, oi.at[1, pl.ds(3, 8), j], l_s.at[5])
    own_x.start()
    own_innov.start()

    flip = mem_of(1 - zl, y)
    other = di + 1 - 2 * core
    remote = lax.rem(di + 15 + 2 * core, 16)
    barrier = pltpu.get_barrier_semaphore()
    for k in range(1, 8):
        pl.semaphore_signal(barrier, inc=1, device_id={"dist": di, "mem": lax.rem(j + k, 8)}, device_id_type=MESH)
    pl.semaphore_signal(barrier, inc=1, device_id={"dist": other, "mem": j}, device_id_type=MESH)
    pl.semaphore_signal(barrier, inc=1, device_id={"dist": remote, "mem": flip}, device_id_type=MESH)
    for d in range(8):
        total[d] = jnp.zeros((256, 1024), jnp.float32)
    pl.semaphore_wait(barrier, 9)

    def remote_copy(source, target, send, recv, dist, mem):
        return pltpu.make_async_remote_copy(
            src_ref=source, dst_ref=target, send_sem=send, recv_sem=recv,
            device_id={"dist": dist, "mem": mem}, device_id_type=MESH)

    def spread_nodes(k, q):
        d = district(q)
        target = mem_of(lax.rem(zl + k // 4, 2), y + k % 4)
        return remote_copy(
            anom.at[d, pl.ds(pl.multiple_of(target * 256, 256), 256), :], xo.at[d, j],
            a_s.at[k - 1, q], a_r.at[k - 1, q], di, target)

    def unit(u):
        middle = (u >= 5) & (u < 11)
        odd = lax.rem(u, 2)
        kind = jnp.where(middle, odd, jnp.where(u < 5, 0, 1))
        q = jnp.where(middle, jnp.where(odd == 1, (u - 5) // 2, 2 + u // 2), jnp.where(u < 5, u, 18 - u))
        return kind, q, district(q), 1 - 2 * lax.rem(u, 2), lax.rem(u, 3) == 2

    def edge_copy(u, edge, source, block, mem):
        return remote_copy(source, block, g_s.at[edge, u], g_r.at[edge, u], di, mem)

    def forward(u, edge):
        kind, q, d, s, three = unit(u)
        here, there = zl, 1 - zl
        from_, to = {
            3: (mem_of(here, y - s), flip),
            4: (mem_of(here, y + s), jnp.where(three, flip, mem_of(here, y - s))),
            5: (jnp.where(three, mem_of(here, y - s), flip), jnp.where(three, mem_of(here, y + s), mem_of(here, y - s))),
            6: (jnp.where(three, mem_of(there, y + s), mem_of(there, y - s)),
                jnp.where(three, mem_of(here, y - s), mem_of(here, y + s))),
        }[edge]
        block = oi.at[kind, 3 + d, from_]
        return edge_copy(u, edge, block, block, to)

    def gathered(u, edge):
        kind, q, d, s, three = unit(u)
        here, there = zl, 1 - zl
        from_ = (
            mem_of(here, y - s),
            mem_of(here, y + s),
            flip,
            mem_of(there, y - s),
            jnp.where(three, mem_of(there, y + s), mem_of(here, y + 2)),
            jnp.where(three, mem_of(here, y + 2), mem_of(there, y + s)),
            mem_of(there, y + 2),
        )[edge]
        block = oi.at[kind, 3 + d, from_]
        return edge_copy(u, edge, block, block, flip)

    def halo(u):
        kind, q, d, s, three = unit(u)
        near = q >= 5
        slot = jnp.where(d >= 5, d - 5, 11 + d)
        index = jnp.where(near, q - 2, q)
        return remote_copy(
            oi.at[kind, 3 + d], oi.at[kind, slot], h_s.at[kind, index], h_r.at[kind, index],
            jnp.where(near, other, remote), jnp.where(near, j, flip))

    def halo_in(kind, index):
        slot = jnp.where(core == 0, jnp.where(index < 3, 2 - index, 16 - index), jnp.where(index < 3, 11 + index, index - 3))
        return remote_copy(oi.at[kind, slot], oi.at[kind, slot], h_s.at[kind, index], h_r.at[kind, index], other, j)

    def has_halo(u):
        q = unit(u)[1]
        return (q < 3) | (q >= 5)

    def own_seen(d):
        return pltpu.make_async_copy(seen.at[d], oi.at[0, 3 + d, j], w_s.at[d])

    for k in FAR_FIRST[:3]:
        spread_nodes(k, NODE_TURN[0]).start()
    for copy in small:
        copy.wait()
    slot8 = lax.broadcasted_iota(jnp.int32, (256, 8), 0)
    cols[...] = jnp.where(slot8 < count[...], node[...].T, -1)
    xy = pos[:, pl.ds(pl.multiple_of(j * 256, 256), 256)].astype(jnp.float32).T
    for d in range(8):
        for axis in range(2):
            spot[axis, d] = jnp.broadcast_to(xy[:, 8 * axis + d:8 * axis + d + 1], (256, 128))

    def observe(q):
        d, n = district(q), q
        load(n).wait()
        lane = lax.broadcasted_iota(jnp.int32, (256, 8), 1)
        which = jnp.sum(jnp.where(lane == d, cols[...], 0), axis=1, keepdims=True)
        hot = jnp.where(lax.broadcasted_iota(jnp.int32, (256, 2048), 1) == which, 1.0, 0.0).astype(jnp.bfloat16)
        rows = jnp.dot(hot, held[lax.rem(n, 2)], preferred_element_type=jnp.float32)
        seen[d] = rows.astype(jnp.bfloat16)
        spots = lax.dot_general(pos[...], hot, (((1,), (1,)), ((), ())), preferred_element_type=jnp.float32)
        row16 = lax.broadcasted_iota(jnp.int32, (16, 256), 0)
        row8 = lax.broadcasted_iota(jnp.int32, (8, 256), 0)
        sx = jnp.sum(jnp.where(row16 == d, spots, 0.0), axis=0, keepdims=True)
        sy = jnp.sum(jnp.where(row16 == d + 8, spots, 0.0), axis=0, keepdims=True)
        sv = jnp.sum(jnp.where(row8 == d, var[...].astype(jnp.float32), 0.0), axis=0, keepdims=True)
        meta[3 + d] = jnp.where(row8 == 0, sx, jnp.where(row8 == 1, sy, jnp.where(row8 == 2, sv, 0.0)))

        @pl.when(n < 6)
        def _():
            load(n + 2).start()

        own_seen(d).start()

    far_meta = remote_copy(
        meta.at[pl.ds(3 + 5 * core, 3)], meta.at[pl.ds(11 - 11 * core, 3)], m_s.at[0], m_r.at[0], remote, flip)
    near_meta = remote_copy(
        meta.at[pl.ds(8 - 5 * core, 3)], meta.at[pl.ds(11 * core, 3)], m_s.at[1], m_r.at[1], other, j)

    def slot_of(qe):
        return 3 + qe + core * (7 - 2 * qe)

    def bring(kind, slot, which):
        @pl.when(kind == 0)
        def _():
            pltpu.make_async_copy(oi.at[0, slot], obs.at[slot], v_s.at[which]).start()

        @pl.when(kind == 1)
        def _():
            pltpu.make_async_copy(oi.at[1, slot], inn.at[slot], v_s.at[which]).start()

    def brought(kind, slot, which):
        @pl.when(kind == 0)
        def _():
            pltpu.make_async_copy(oi.at[0, slot], obs.at[slot], v_s.at[which]).wait()
            square = jnp.zeros((256, 128), jnp.float32)
            for m in range(8):
                part = obs[slot, m].astype(jnp.float32)
                square = square + part * part
            square = jnp.sum(square.T, axis=0, keepdims=True)
            inv[pl.ds(slot, 1)] = 1.0 / (square + 1023.0 * meta[slot, 2:3])

        @pl.when(kind == 1)
        def _():
            pltpu.make_async_copy(oi.at[1, slot], inn.at[slot], v_s.at[which]).wait()

    def own_event(t, act):
        u = t - 3 * LAG

        @pl.when((u >= 0) & (u < OWN_USED))
        def _():
            kind, q, d, s, three = unit(u)
            act(kind, 3 + d, 0)

    def near_event(t, act, first):
        u = t - 3 * LAG - 1

        @pl.when((u == 6) | (u == 8) | ((u >= 10) & (u < 14)))
        def _():
            kind, q, d, s, three = unit(u)
            if first:
                halo_in(kind, q - 2).wait_recv()
            act(kind, slot_of(15 - q), 1)

    def far_event(t, act, first):
        early = t < 15
        i = jnp.where(early, t - 10, t - 15) // 2

        @pl.when((t == 10) | (t == 12) | (t == 14) | (t == 15) | (t == 17) | (t == 19))
        def _():
            kind = jnp.where(early, 0, 1)
            if first:
                halo_in(kind, i).wait_recv()
            act(kind, slot_of(-1 - i), 2)

    def nodes_copy(q):
        return pltpu.make_async_copy(xo.at[district(q)], xs.at[district(q)], x_s)

    def nodes_turn(t):
        turn = t // 2 - 2
        return (turn >= 0) & (turn < 8), jnp.where(turn < 2, 1 - turn, turn)

    def nodes_arrive(t):
        due, q = nodes_turn(t)

        @pl.when(t == 4)
        def _():
            own_x.wait()

        @pl.when(due & (lax.rem(t, 2) == 0))
        def _():
            d = district(q)
            for k in range(1, 8):
                source = mem_of(lax.rem(zl + k // 4, 2), y + 4 - k % 4)
                block = xo.at[d, source]
                remote_copy(block, block, a_s.at[k - 1, q], a_r.at[k - 1, q], di, flip).wait_recv()
            nodes_copy(q).start()

    def nodes_ready(t):
        due, q = nodes_turn(t)

        @pl.when(due & (lax.rem(t, 2) == 1))
        def _():
            nodes_copy(q).wait()

    def tasks(t, table, first):
        code = jnp.int32(0)
        for i, word in enumerate(table):
            if word:
                code = jnp.where(t == first + i, word, code)
        return code

    def places(code, i):
        item = lax.rem(code // (128 ** i), 128)
        d, slot = district(lax.rem(item, 8)), slot_of(item // 8 - 3)
        return d, slot, slot - d

    def joined(ref, index):
        return jnp.concatenate([ref[index, m] for m in range(8)], axis=1)

    def gain_block(t, part):
        code = tasks(t, GAIN_TABLE, GAIN_FIRST)

        @pl.when((t >= GAIN_FIRST) & (t < GAIN_FIRST + len(GAIN_TABLE)))
        def _():
            for i in part:
                d, slot, s = places(code, i)
                cov = lax.dot_general(joined(xs, d), joined(obs, slot), (((1,), (1,)), ((), ())), preferred_element_type=jnp.float32)
                row = inv[pl.ds(slot, 1)] * flags[d, s].astype(jnp.float32)
                node_x, node_y = spot[0, d], spot[1, d]
                weight = taper(
                    jnp.concatenate([node_x, node_x], axis=1), jnp.concatenate([node_y, node_y], axis=1),
                    meta[slot], (s - RADIUS).astype(jnp.float32))
                gains[d, s] = (weight * cov * row).astype(jnp.bfloat16)

    def increment_block(t):
        code = tasks(t, INC_TABLE, INC_FIRST)

        @pl.when(code > 0)
        def _():
            for i in range(4):
                d, slot, s = places(code, i)
                total[d] += jnp.dot(gains[d, s], joined(inn, slot), preferred_element_type=jnp.float32)

    def hand_over(last):
        copies = []
        for q, others in enumerate(LATE):
            for r, e in enumerate(others):
                if ((e, q) in LAST_GAINS) != last:
                    continue
                d = district(q)
                copies.append(pltpu.make_async_copy(gains.at[d, slot_of(e) - d], late.at[d, r], f_s.at[q, r]))
        return copies

    def finish(q):
        d = district(q)
        return pltpu.make_async_copy(total.at[d], out.at[d], o_s.at[q])

    def step(t, carry):
        @pl.when(t < UNITS)
        def _():
            kind, q, d, s, three = unit(t)
            targets = (mem_of(zl, y + s), mem_of(zl, y - s), flip)

            @pl.when(kind == 0)
            def _():
                observe(q)
                for edge in range(3):
                    edge_copy(t, edge, seen.at[d], oi.at[0, 3 + d, j], targets[edge]).start()

            @pl.when(kind == 1)
            def _():
                for edge in range(3):
                    edge_copy(t, edge, innov.at[d], oi.at[1, 3 + d, j], targets[edge]).start()

        turn = t // 2
        place = jnp.where(turn < 2, 1 - turn, turn)

        @pl.when((t >= 1) & (t < 16) & (lax.rem(t, 2) == 0))
        def _():
            for k in FAR_FIRST[:3]:
                spread_nodes(k, place).start()

        @pl.when((t < 16) & (lax.rem(t, 2) == 1))
        def _():
            for k in FAR_FIRST[3:]:
                spread_nodes(k, place).start()

        @pl.when(t == 3)
        def _():
            far_meta.start()

        @pl.when(t == 9)
        def _():
            far_meta.wait_recv()

        @pl.when(t == 11)
        def _():
            near_meta.start()

        @pl.when(t == 13)
        def _():
            near_meta.wait_recv()


        own_event(t - 1, brought)
        near_event(t - 1, brought, False)
        far_event(t - 1, brought, False)
        nodes_ready(t)

        u = t - LAG

        @pl.when((u >= 0) & (u < UNITS))
        def _():
            for edge in range(3):
                gathered(u, edge).wait_recv()
                forward(u, edge + 3).start()

        v = t - 2 * LAG

        @pl.when((v >= 0) & (v < UNITS))
        def _():
            gathered_last(v, True)
            forward(v, 6).start()

        @pl.when(t == STEPS - 1)
        def _():
            for copy in hand_over(False):
                copy.start()
            for q in range(8):
                finish(q).start()

        w = t - 3 * LAG

        @pl.when((w >= 0) & (w < UNITS))
        def _():
            gathered_last(w, False)
            gathered(w, 5).wait_recv()
            gathered(w, 6).wait_recv()
            kind, q, d, s, three = unit(w)

            @pl.when(kind == 0)
            def _():
                own_seen(d).wait()

            @pl.when(w == 3)
            def _():
                own_innov.wait()

            @pl.when(has_halo(w))
            def _():
                halo(w).start()

        own_event(t, bring)
        near_event(t, bring, True)
        far_event(t, bring, True)
        nodes_arrive(t)
        gain_block(t, (0, 1, 2, 3))
        increment_block(t)
        return carry

    def gathered_last(u, first):
        three = unit(u)[4]
        take4 = three if first else jnp.logical_not(three)

        @pl.when(take4)
        def _():
            gathered(u, 4).wait_recv()

        @pl.when(jnp.logical_not(take4))
        def _():
            gathered(u, 3).wait_recv()

    lax.fori_loop(0, STEPS, step, 0)
    for copy in hand_over(True):
        copy.start()

    def drain(u, carry):
        for edge in range(7):
            gathered(u, edge).wait_send()

        @pl.when(has_halo(u))
        def _():
            halo(u).wait_send()

        return carry

    lax.fori_loop(0, UNITS, drain, 0)

    def drain_nodes(q, carry):
        for k in range(1, 8):
            spread_nodes(k, q).wait_send()
        return carry

    lax.fori_loop(0, 8, drain_nodes, 0)
    far_meta.wait_send()
    near_meta.wait_send()
    for q in range(8):
        finish(q).wait()
    for copy in hand_over(False) + hand_over(True):
        copy.wait()


def taper(node_x, node_y, meta, shift):
    dx = (meta[0:1] + shift) - node_x
    dy = meta[1:2] - node_y
    square = jnp.maximum((dx * dx + dy * dy) * (1.0 / (REACH * REACH)), 1e-30)
    root = lax.rsqrt(square)
    z = square * root
    inner = (((-0.25 * z + 0.5) * z + 0.625) * z - 5.0 / 3.0) * square + 1.0
    left = jnp.maximum(2.0 - z, 0.0)
    left = left * left
    outer = (left * left) * (z * (1.0 / 12.0) + (1.0 / 6.0) - root * (1.0 / 24.0))
    return jnp.where(z < 1.0, inner, outer)


def analysis(anomalies, innovations, obs_var, node_pos, obs_node, obs_count, in_radius):
    bf16, f32 = jnp.bfloat16, jnp.float32
    return pl.pallas_call(
        analysis_kernel,
        out_shape=(
            jax.ShapeDtypeStruct((8, 256, 1024), f32),
            jax.ShapeDtypeStruct((8, MOST, 256, 256), bf16),
            jax.ShapeDtypeStruct((8, 8, 256, 128), bf16),
            jax.ShapeDtypeStruct((2, 14, 8, 256, 128), bf16),
        ),
        in_specs=[HBM] * 6 + [SMEM],
        out_specs=(HBM,) * 4,
        scratch_shapes=[
            pltpu.VMEM((2, 2048, 128), bf16),
            pltpu.VMEM((8, 256, 128), bf16),
            pltpu.VMEM((14, 8, 256), f32),
            pltpu.VMEM((8, 256), jnp.int32),
            pltpu.VMEM((1, 8), jnp.int32),
            pltpu.VMEM((16, 2048), bf16),
            pltpu.VMEM((8, 256), bf16),
            pltpu.VMEM((256, 8), jnp.int32),
            pltpu.VMEM((8, 8, 256, 128), bf16),
            pltpu.VMEM((14, 8, 256, 128), bf16),
            pltpu.VMEM((14, 8, 256, 128), bf16),
            pltpu.VMEM((8, 7, 256, 256), bf16),
            pltpu.VMEM((8, 256, 1024), f32),
            pltpu.VMEM((14, 256), f32),
            pltpu.VMEM((2, 8, 256, 128), f32),
            DMA((7, 8)), DMA((7, 8)), DMA((7, UNITS)), DMA((7, UNITS)), DMA((2, 6)), DMA((2, 6)), DMA((2,)), DMA((2,)),
            DMA((6,)), DMA((2,)), DMA((8,)), DMA((3,)), DMA, DMA((8,)), DMA((8, MOST)),
        ],
        compiler_params=pltpu.CompilerParams(collective_id=0, has_side_effects=True, vmem_limit_bytes=58 << 20),
    )(anomalies, innovations, obs_node, obs_count.reshape(1, 8), node_pos.reshape(16, 2048), obs_var, in_radius)


def closing_kernel(flags, total_h, late_h, oi, out, total, gains, inn, i_s, g_s, t_s):
    d = pl.program_id(0)
    core = lax.rem(lax.axis_index("dist"), 2)

    def slot_of(qe):
        return 3 + qe + core * (7 - 2 * qe)

    used = sorted({e for others in LATE for e in others})
    innovations = [
        pltpu.make_async_copy(oi.at[1, slot_of(e)], inn.at[slot_of(e)], i_s.at[i]) for i, e in enumerate(used)]

    def sums(i):
        return pltpu.make_async_copy(total_h.at[i], total.at[i], t_s.at[i])

    def weights(i, r):
        return pltpu.make_async_copy(late_h.at[i, r], gains.at[i, r], g_s.at[i, r])

    @pl.when(d == 0)
    def _():
        for i in range(8):
            sums(i).start()
            for r in range(MOST):
                counts = [len(others) > r for others in LATE]

                @pl.when(jnp.where(core == 0, int(counts[i]), int(counts[7 - i])) > 0)
                def _():
                    weights(i, r).start()
            if i == 0:
                for copy in innovations:
                    copy.start()

    sums(d).wait()
    out[0] = total[d]

    @pl.when(d == 0)
    def _():
        for copy in innovations:
            copy.wait()

    q = d + core * (7 - 2 * d)
    code = jnp.int32(0)
    for place, others in enumerate(LATE):
        code = jnp.where(q == place, sum((e + 4) * 16 ** r for r, e in enumerate(others)), code)

    def add(r, code):
        item = lax.rem(code, 16)
        slot = slot_of(item - 4)
        s = jnp.clip(slot - d, 0, 6)

        @pl.when(item > 0)
        def _():
            weights(d, r).wait()

        @pl.when((item > 0) & (flags[d, s] > 0))
        def _():
            rows = jnp.concatenate([inn[slot, m] for m in range(8)], axis=1)
            out[0] += jnp.dot(gains[d, r], rows, preferred_element_type=jnp.float32)

        return code // 16

    lax.fori_loop(0, MOST, add, code)


def closing(in_radius, total, late, oi):
    used = len({e for others in LATE for e in others})
    block = pl.BlockSpec((1, 256, 1024), lambda d: (d, 0, 0))
    return pl.pallas_call(
        closing_kernel,
        grid=(8,),
        out_shape=jax.ShapeDtypeStruct((8, 256, 1024), jnp.float32),
        in_specs=[SMEM, HBM, HBM, HBM],
        out_specs=block,
        scratch_shapes=[
            pltpu.VMEM((8, 256, 1024), jnp.float32),
            pltpu.VMEM((8, MOST, 256, 256), jnp.bfloat16),
            pltpu.VMEM((14, 8, 256, 128), jnp.bfloat16),
            DMA((used,)),
            DMA((8, MOST)),
            DMA((8,)),
        ],
        compiler_params=pltpu.CompilerParams(vmem_limit_bytes=56 << 20),
    )(in_radius, total, late, oi)


def on_device(*arrays):
    total, late, xo, oi = analysis(*arrays)
    return closing(arrays[-1], total, late, oi)


def solution(mesh):
    return jax.shard_map(
        on_device,
        mesh=mesh,
        in_specs=(
            P("dist", None, "mem"),
            P("dist", None, "mem"),
            P("dist", None),
            P(None, "dist", None),
            P("dist", None),
            P("dist"),
            P("dist", None),
        ),
        out_specs=P("dist", "mem", None),
        check_vma=False,
    )
```

```python
import jax
import jax.numpy as jnp
from jax import lax
from jax.experimental import pallas as pl
from jax.experimental.pallas import tpu as pltpu
from jax.sharding import PartitionSpec as P

MESH = pl.DeviceIdType.MESH
HBM = pl.BlockSpec(memory_space=pltpu.HBM)
VMEM = pl.BlockSpec(memory_space=pltpu.VMEM)
SMEM = pl.BlockSpec(memory_space=pltpu.SMEM)
DMA = pltpu.SemaphoreType.DMA
RADIUS = 3
REACH = 2.5
UNITS = 16
LAG = 2
FAR_FIRST = (6, 2, 5, 7, 4, 1, 3)
STEPS = 22
OWN_USED = 14
NODE_TURN = (1, 0, 2, 3, 4, 5, 6, 7)


def column(*pairs):
    return sum(((e + 3) * 8 + d) * 128 ** i for i, (e, d) in enumerate(pairs))


GAIN_FIRST = 8
GAIN_TABLE = (
    column((0, 0), (0, 1), (1, 0), (1, 1)),
    column((0, 2), (1, 2), (2, 0), (2, 1)),
    column((2, 2), (3, 0), (3, 1), (3, 2)),
    column((0, 3), (1, 3), (-1, 0), (-1, 1)),
    column((-1, 2), (2, 3), (4, 1), (4, 2)),
    column((1, 4), (2, 4), (-2, 0), (-2, 1)),
    column((5, 2), (5, 3), (5, 4), (4, 3)),
    column((2, 5), (6, 3), (6, 4), (6, 5)),
    column((-3, 0), (5, 5), (4, 4), (4, 5)),
    column((7, 4), (7, 5), (7, 6), (6, 6)),
    column((8, 5), (8, 6), (5, 6), (9, 6)),
    column((7, 7), (6, 7), (8, 7), (5, 7)),
    column((9, 7), (4, 6), (4, 7), (10, 7)),
    column((3, 3), (3, 4), (3, 5), (3, 6)),
)
INC_FIRST = 12
INC_TABLE = (
    column((0, 0), (0, 1), (0, 2), (0, 3)),
    0,
    column((1, 0), (1, 1), (1, 2), (1, 3)),
    0,
    column((1, 4), (2, 0), (2, 1), (2, 2)),
    column((-1, 0), (-1, 1), (-1, 2), (2, 3)),
    column((2, 4), (2, 5), (-2, 0), (-2, 1)),
    column((7, 4), (7, 5), (7, 6), (7, 7)),
    column((6, 3), (6, 4), (6, 5), (6, 6)),
)
LATE = (
    (-3, 3,),
    (3, 4,),
    (3, 4, 5,),
    (3, 4, 5,),
    (3, 4, 5,),
    (3, 4, 5, 8,),
    (3, 4, 5, 8, 9,),
    (4, 5, 6, 8, 9, 10,),
)


LAST_GAINS = ((3, 3), (3, 4), (3, 5), (3, 6))
MOST = max(len(others) for others in LATE)


def analysis_kernel(
    anom, innov, node_h, count_h, pos_h, var_h, flags, out, late, xo, oi,
    held, seen, meta, node, count, pos, var, cols, xs, obs, inn, gains, total, inv, spot,
    a_s, a_r, g_s, g_r, h_s, h_r, m_s, m_r, l_s, p_s, w_s, v_s, x_s, o_s, f_s,
):
    di, j = lax.axis_index("dist"), lax.axis_index("mem")
    core = lax.rem(di, 2)
    zl, y = j // 4, lax.rem(j, 4)

    def mem_of(z, row):
        return z * 4 + lax.rem(row + 8, 4)

    def district(q):
        return q + core * (7 - 2 * q)

    small = [
        pltpu.make_async_copy(node_h, node, l_s.at[0]),
        pltpu.make_async_copy(count_h, count, l_s.at[1]),
        pltpu.make_async_copy(pos_h, pos, l_s.at[2]),
        pltpu.make_async_copy(var_h, var, l_s.at[3]),
    ]
    for copy in small:
        copy.start()

    def load(n):
        return pltpu.make_async_copy(anom.at[district(n)], held.at[lax.rem(n, 2)], p_s.at[lax.rem(n, 2)])

    load(0).start()
    load(1).start()
    take_x = pltpu.make_async_copy(anom.at[:, pl.ds(pl.multiple_of(j * 256, 256), 256), :], xs.at[:, j], l_s.at[4])
    take_innov = pltpu.make_async_copy(innov, inn.at[pl.ds(3, 8), j], l_s.at[5])
    own_x = pltpu.make_async_copy(xs.at[:, j], xo.at[:, j], l_s.at[4])
    own_innov = pltpu.make_async_copy(inn.at[pl.ds(3, 8), j], oi.at[1, pl.ds(3, 8), j], l_s.at[5])
    take_x.start()
    take_innov.start()

    flip = mem_of(1 - zl, y)
    other = di + 1 - 2 * core
    remote = lax.rem(di + 15 + 2 * core, 16)
    barrier = pltpu.get_barrier_semaphore()
    for k in range(1, 8):
        pl.semaphore_signal(barrier, inc=1, device_id={"dist": di, "mem": lax.rem(j + k, 8)}, device_id_type=MESH)
    pl.semaphore_signal(barrier, inc=1, device_id={"dist": other, "mem": j}, device_id_type=MESH)
    pl.semaphore_signal(barrier, inc=1, device_id={"dist": remote, "mem": flip}, device_id_type=MESH)
    for d in range(8):
        total[d] = jnp.zeros((256, 1024), jnp.float32)
    pl.semaphore_wait(barrier, 9)

    def remote_copy(source, target, send, recv, dist, mem):
        return pltpu.make_async_remote_copy(
            src_ref=source, dst_ref=target, send_sem=send, recv_sem=recv,
            device_id={"dist": dist, "mem": mem}, device_id_type=MESH)

    def spread_nodes(k, q):
        d = district(q)
        target = mem_of(lax.rem(zl + k // 4, 2), y + k % 4)
        return remote_copy(
            anom.at[d, pl.ds(pl.multiple_of(target * 256, 256), 256), :], xo.at[d, j],
            a_s.at[k - 1, q], a_r.at[k - 1, q], di, target)

    def unit(u):
        middle = (u >= 5) & (u < 11)
        odd = lax.rem(u, 2)
        kind = jnp.where(middle, odd, jnp.where(u < 5, 0, 1))
        q = jnp.where(middle, jnp.where(odd == 1, (u - 5) // 2, 2 + u // 2), jnp.where(u < 5, u, 18 - u))
        return kind, q, district(q), 1 - 2 * lax.rem(u, 2), lax.rem(u, 3) == 2

    def edge_copy(u, edge, source, block, mem):
        return remote_copy(source, block, g_s.at[edge, u], g_r.at[edge, u], di, mem)

    def forward(u, edge):
        kind, q, d, s, three = unit(u)
        here, there = zl, 1 - zl
        from_, to = {
            3: (mem_of(here, y - s), flip),
            4: (mem_of(here, y + s), jnp.where(three, flip, mem_of(here, y - s))),
            5: (jnp.where(three, mem_of(here, y - s), flip), jnp.where(three, mem_of(here, y + s), mem_of(here, y - s))),
            6: (jnp.where(three, mem_of(there, y + s), mem_of(there, y - s)),
                jnp.where(three, mem_of(here, y - s), mem_of(here, y + s))),
        }[edge]
        block = oi.at[kind, 3 + d, from_]
        return edge_copy(u, edge, block, block, to)

    def gathered(u, edge):
        kind, q, d, s, three = unit(u)
        here, there = zl, 1 - zl
        from_ = (
            mem_of(here, y - s),
            mem_of(here, y + s),
            flip,
            mem_of(there, y - s),
            jnp.where(three, mem_of(there, y + s), mem_of(here, y + 2)),
            jnp.where(three, mem_of(here, y + 2), mem_of(there, y + s)),
            mem_of(there, y + 2),
        )[edge]
        block = oi.at[kind, 3 + d, from_]
        return edge_copy(u, edge, block, block, flip)

    def halo(u):
        kind, q, d, s, three = unit(u)
        near = q >= 5
        slot = jnp.where(d >= 5, d - 5, 11 + d)
        index = jnp.where(near, q - 2, q)
        return remote_copy(
            oi.at[kind, 3 + d], oi.at[kind, slot], h_s.at[kind, index], h_r.at[kind, index],
            jnp.where(near, other, remote), jnp.where(near, j, flip))

    def halo_in(kind, index):
        slot = jnp.where(core == 0, jnp.where(index < 3, 2 - index, 16 - index), jnp.where(index < 3, 11 + index, index - 3))
        return remote_copy(oi.at[kind, slot], oi.at[kind, slot], h_s.at[kind, index], h_r.at[kind, index], other, j)

    def has_halo(u):
        q = unit(u)[1]
        return (q < 3) | (q >= 5)

    def own_seen(d):
        return pltpu.make_async_copy(seen.at[d], oi.at[0, 3 + d, j], w_s.at[d])

    for k in FAR_FIRST[:3]:
        spread_nodes(k, NODE_TURN[0]).start()
    for copy in small + [take_x, take_innov]:
        copy.wait()
    own_x.start()
    own_innov.start()
    slot8 = lax.broadcasted_iota(jnp.int32, (256, 8), 0)
    cols[...] = jnp.where(slot8 < count[...], node[...].T, -1)
    xy = pos[:, pl.ds(pl.multiple_of(j * 256, 256), 256)].astype(jnp.float32).T
    for d in range(8):
        for axis in range(2):
            spot[axis, d] = jnp.broadcast_to(xy[:, 8 * axis + d:8 * axis + d + 1], (256, 128))

    def observe(q):
        d, n = district(q), q
        load(n).wait()
        lane = lax.broadcasted_iota(jnp.int32, (256, 8), 1)
        which = jnp.sum(jnp.where(lane == d, cols[...], 0), axis=1, keepdims=True)
        hot = jnp.where(lax.broadcasted_iota(jnp.int32, (256, 2048), 1) == which, 1.0, 0.0).astype(jnp.bfloat16)
        rows = jnp.dot(hot, held[lax.rem(n, 2)], preferred_element_type=jnp.float32)
        seen[d] = rows.astype(jnp.bfloat16)
        spots = lax.dot_general(pos[...], hot, (((1,), (1,)), ((), ())), preferred_element_type=jnp.float32)
        row16 = lax.broadcasted_iota(jnp.int32, (16, 256), 0)
        row8 = lax.broadcasted_iota(jnp.int32, (8, 256), 0)
        sx = jnp.sum(jnp.where(row16 == d, spots, 0.0), axis=0, keepdims=True)
        sy = jnp.sum(jnp.where(row16 == d + 8, spots, 0.0), axis=0, keepdims=True)
        sv = jnp.sum(jnp.where(row8 == d, var[...].astype(jnp.float32), 0.0), axis=0, keepdims=True)
        meta[3 + d] = jnp.where(row8 == 0, sx, jnp.where(row8 == 1, sy, jnp.where(row8 == 2, sv, 0.0)))

        @pl.when(n < 6)
        def _():
            load(n + 2).start()

        own_seen(d).start()

    far_meta = remote_copy(
        meta.at[pl.ds(3 + 5 * core, 3)], meta.at[pl.ds(11 - 11 * core, 3)], m_s.at[0], m_r.at[0], remote, flip)
    near_meta = remote_copy(
        meta.at[pl.ds(8 - 5 * core, 3)], meta.at[pl.ds(11 * core, 3)], m_s.at[1], m_r.at[1], other, j)

    def slot_of(qe):
        return 3 + qe + core * (7 - 2 * qe)

    def bring(kind, slot, which):
        @pl.when(kind == 0)
        def _():
            pltpu.make_async_copy(oi.at[0, slot], obs.at[slot], v_s.at[which]).start()

        @pl.when(kind == 1)
        def _():
            pltpu.make_async_copy(oi.at[1, slot], inn.at[slot], v_s.at[which]).start()

    def brought(kind, slot, which):
        @pl.when(kind == 0)
        def _():
            pltpu.make_async_copy(oi.at[0, slot], obs.at[slot], v_s.at[which]).wait()
            square = jnp.zeros((256, 128), jnp.float32)
            for m in range(8):
                part = obs[slot, m].astype(jnp.float32)
                square = square + part * part
            square = jnp.sum(square.T, axis=0, keepdims=True)
            inv[pl.ds(slot, 1)] = 1.0 / (square + 1023.0 * meta[slot, 2:3])

        @pl.when(kind == 1)
        def _():
            pltpu.make_async_copy(oi.at[1, slot], inn.at[slot], v_s.at[which]).wait()

    def own_event(t, act):
        u = t - 3 * LAG

        @pl.when((u >= 0) & (u < OWN_USED))
        def _():
            kind, q, d, s, three = unit(u)
            act(kind, 3 + d, 0)

    def near_event(t, act, first):
        u = t - 3 * LAG - 1

        @pl.when((u == 6) | (u == 8) | ((u >= 10) & (u < 14)))
        def _():
            kind, q, d, s, three = unit(u)
            if first:
                halo_in(kind, q - 2).wait_recv()
            act(kind, slot_of(15 - q), 1)

    def far_event(t, act, first):
        early = t < 15
        i = jnp.where(early, t - 10, t - 15) // 2

        @pl.when((t == 10) | (t == 12) | (t == 14) | (t == 15) | (t == 17) | (t == 19))
        def _():
            kind = jnp.where(early, 0, 1)
            if first:
                halo_in(kind, i).wait_recv()
            act(kind, slot_of(-1 - i), 2)

    def nodes_copy(q):
        return pltpu.make_async_copy(xo.at[district(q)], xs.at[district(q)], x_s)

    def nodes_turn(t):
        turn = t // 2 - 2
        return (turn >= 0) & (turn < 8), jnp.where(turn < 2, 1 - turn, turn)

    def nodes_arrive(t):
        due, q = nodes_turn(t)

        @pl.when(t == 4)
        def _():
            own_x.wait()

        @pl.when(due & (lax.rem(t, 2) == 0))
        def _():
            d = district(q)
            for k in range(1, 8):
                source = mem_of(lax.rem(zl + k // 4, 2), y + 4 - k % 4)
                block = xo.at[d, source]
                remote_copy(block, block, a_s.at[k - 1, q], a_r.at[k - 1, q], di, flip).wait_recv()
            nodes_copy(q).start()

    def nodes_ready(t):
        due, q = nodes_turn(t)

        @pl.when(due & (lax.rem(t, 2) == 1))
        def _():
            nodes_copy(q).wait()

    def tasks(t, table, first):
        code = jnp.int32(0)
        for i, word in enumerate(table):
            if word:
                code = jnp.where(t == first + i, word, code)
        return code

    def places(code, i):
        item = lax.rem(code // (128 ** i), 128)
        d, slot = district(lax.rem(item, 8)), slot_of(item // 8 - 3)
        return d, slot, slot - d

    def joined(ref, index):
        return jnp.concatenate([ref[index, m] for m in range(8)], axis=1)

    def gain_block(t, part):
        code = tasks(t, GAIN_TABLE, GAIN_FIRST)

        @pl.when((t >= GAIN_FIRST) & (t < GAIN_FIRST + len(GAIN_TABLE)))
        def _():
            for i in part:
                d, slot, s = places(code, i)
                cov = lax.dot_general(joined(xs, d), joined(obs, slot), (((1,), (1,)), ((), ())), preferred_element_type=jnp.float32)
                row = inv[pl.ds(slot, 1)] * flags[d, s].astype(jnp.float32)
                node_x, node_y = spot[0, d], spot[1, d]
                weight = taper(
                    jnp.concatenate([node_x, node_x], axis=1), jnp.concatenate([node_y, node_y], axis=1),
                    meta[slot], (s - RADIUS).astype(jnp.float32))
                gains[d, s] = (weight * cov * row).astype(jnp.bfloat16)

    def increment_block(t):
        code = tasks(t, INC_TABLE, INC_FIRST)

        @pl.when(code > 0)
        def _():
            for i in range(4):
                d, slot, s = places(code, i)
                total[d] += jnp.dot(gains[d, s], joined(inn, slot), preferred_element_type=jnp.float32)

    def hand_over(last):
        copies = []
        for q, others in enumerate(LATE):
            for r, e in enumerate(others):
                if ((e, q) in LAST_GAINS) != last:
                    continue
                d = district(q)
                copies.append(pltpu.make_async_copy(gains.at[d, slot_of(e) - d], late.at[d, r], f_s.at[q, r]))
        return copies

    def finish(q):
        d = district(q)
        return pltpu.make_async_copy(total.at[d], out.at[d], o_s.at[q])

    def step(t, carry):
        @pl.when(t < UNITS)
        def _():
            kind, q, d, s, three = unit(t)
            targets = (mem_of(zl, y + s), mem_of(zl, y - s), flip)

            @pl.when(kind == 0)
            def _():
                observe(q)
                for edge in range(3):
                    edge_copy(t, edge, seen.at[d], oi.at[0, 3 + d, j], targets[edge]).start()

            @pl.when(kind == 1)
            def _():
                for edge in range(3):
                    edge_copy(t, edge, innov.at[d], oi.at[1, 3 + d, j], targets[edge]).start()

        @pl.when(t == 3)
        def _():
            far_meta.start()

        @pl.when(t == 9)
        def _():
            far_meta.wait_recv()

        @pl.when(t == 11)
        def _():
            near_meta.start()

        @pl.when(t == 13)
        def _():
            near_meta.wait_recv()


        own_event(t - 1, brought)
        near_event(t - 1, brought, False)
        far_event(t - 1, brought, False)
        nodes_ready(t)

        u = t - LAG

        @pl.when((u >= 0) & (u < UNITS))
        def _():
            for edge in range(3):
                gathered(u, edge).wait_recv()
                forward(u, edge + 3).start()

        v = t - 2 * LAG

        @pl.when((v >= 0) & (v < UNITS))
        def _():
            gathered_last(v, True)
            forward(v, 6).start()

        @pl.when(t == STEPS - 1)
        def _():
            for copy in hand_over(False):
                copy.start()
            for q in range(8):
                finish(q).start()

        turn = t // 2
        place = jnp.where(turn < 2, 1 - turn, turn)

        @pl.when((t >= 1) & (t < 16) & (lax.rem(t, 2) == 0))
        def _():
            for k in FAR_FIRST[:3]:
                spread_nodes(k, place).start()

        @pl.when((t < 16) & (lax.rem(t, 2) == 1))
        def _():
            for k in FAR_FIRST[3:]:
                spread_nodes(k, place).start()

        w = t - 3 * LAG

        @pl.when((w >= 0) & (w < UNITS))
        def _():
            gathered_last(w, False)
            gathered(w, 5).wait_recv()
            gathered(w, 6).wait_recv()
            kind, q, d, s, three = unit(w)

            @pl.when(kind == 0)
            def _():
                own_seen(d).wait()

            @pl.when(w == 3)
            def _():
                own_innov.wait()

            @pl.when(has_halo(w))
            def _():
                halo(w).start()

        own_event(t, bring)
        near_event(t, bring, True)
        far_event(t, bring, True)
        nodes_arrive(t)
        gain_block(t, (0, 1, 2, 3))
        increment_block(t)
        return carry

    def gathered_last(u, first):
        three = unit(u)[4]
        take4 = three if first else jnp.logical_not(three)

        @pl.when(take4)
        def _():
            gathered(u, 4).wait_recv()

        @pl.when(jnp.logical_not(take4))
        def _():
            gathered(u, 3).wait_recv()

    lax.fori_loop(0, STEPS, step, 0)
    for copy in hand_over(True):
        copy.start()

    def drain(u, carry):
        for edge in range(7):
            gathered(u, edge).wait_send()

        @pl.when(has_halo(u))
        def _():
            halo(u).wait_send()

        return carry

    lax.fori_loop(0, UNITS, drain, 0)

    def drain_nodes(q, carry):
        for k in range(1, 8):
            spread_nodes(k, q).wait_send()
        return carry

    lax.fori_loop(0, 8, drain_nodes, 0)
    far_meta.wait_send()
    near_meta.wait_send()
    for q in range(8):
        finish(q).wait()
    for copy in hand_over(False) + hand_over(True):
        copy.wait()


def taper(node_x, node_y, meta, shift):
    dx = (meta[0:1] + shift) - node_x
    dy = meta[1:2] - node_y
    square = jnp.maximum((dx * dx + dy * dy) * (1.0 / (REACH * REACH)), 1e-30)
    root = lax.rsqrt(square)
    z = square * root
    inner = (((-0.25 * z + 0.5) * z + 0.625) * z - 5.0 / 3.0) * square + 1.0
    left = jnp.maximum(2.0 - z, 0.0)
    left = left * left
    outer = (left * left) * (z * (1.0 / 12.0) + (1.0 / 6.0) - root * (1.0 / 24.0))
    return jnp.where(z < 1.0, inner, outer)


def analysis(anomalies, innovations, obs_var, node_pos, obs_node, obs_count, in_radius):
    bf16, f32 = jnp.bfloat16, jnp.float32
    return pl.pallas_call(
        analysis_kernel,
        out_shape=(
            jax.ShapeDtypeStruct((8, 256, 1024), f32),
            jax.ShapeDtypeStruct((8, MOST, 256, 256), bf16),
            jax.ShapeDtypeStruct((8, 8, 256, 128), bf16),
            jax.ShapeDtypeStruct((2, 14, 8, 256, 128), bf16),
        ),
        in_specs=[HBM] * 6 + [SMEM],
        out_specs=(HBM,) * 4,
        scratch_shapes=[
            pltpu.VMEM((2, 2048, 128), bf16),
            pltpu.VMEM((8, 256, 128), bf16),
            pltpu.VMEM((14, 8, 256), f32),
            pltpu.VMEM((8, 256), jnp.int32),
            pltpu.VMEM((1, 8), jnp.int32),
            pltpu.VMEM((16, 2048), bf16),
            pltpu.VMEM((8, 256), bf16),
            pltpu.VMEM((256, 8), jnp.int32),
            pltpu.VMEM((8, 8, 256, 128), bf16),
            pltpu.VMEM((14, 8, 256, 128), bf16),
            pltpu.VMEM((14, 8, 256, 128), bf16),
            pltpu.VMEM((8, 7, 256, 256), bf16),
            pltpu.VMEM((8, 256, 1024), f32),
            pltpu.VMEM((14, 256), f32),
            pltpu.VMEM((2, 8, 256, 128), f32),
            DMA((7, 8)), DMA((7, 8)), DMA((7, UNITS)), DMA((7, UNITS)), DMA((2, 6)), DMA((2, 6)), DMA((2,)), DMA((2,)),
            DMA((6,)), DMA((2,)), DMA((8,)), DMA((3,)), DMA, DMA((8,)), DMA((8, MOST)),
        ],
        compiler_params=pltpu.CompilerParams(collective_id=0, has_side_effects=True, vmem_limit_bytes=58 << 20),
    )(anomalies, innovations, obs_node, obs_count.reshape(1, 8), node_pos.reshape(16, 2048), obs_var, in_radius)


def closing_kernel(flags, total_h, late_h, oi, out, total, gains, inn, i_s, g_s, t_s, o_s):
    core = lax.rem(lax.axis_index("dist"), 2)

    def slot_of(qe):
        return 3 + qe + core * (7 - 2 * qe)

    used = sorted({e for others in LATE for e in others})
    innovations = [
        pltpu.make_async_copy(oi.at[1, slot_of(e)], inn.at[slot_of(e)], i_s.at[i]) for i, e in enumerate(used)]

    def sums(d):
        return pltpu.make_async_copy(total_h.at[d], total.at[d], t_s.at[d])

    def result(d):
        return pltpu.make_async_copy(total.at[d], out.at[d], o_s.at[d])

    def weights(d, r):
        return pltpu.make_async_copy(late_h.at[d, r], gains.at[d, r], g_s.at[d, r])

    def each(d, act):
        q = d + core * (7 - 2 * d)
        code = jnp.int32(0)
        for place, others in enumerate(LATE):
            code = jnp.where(q == place, sum((e + 4) * 16 ** r for r, e in enumerate(others)), code)

        def one(r, code):
            item = lax.rem(code, 16)
            slot = jnp.clip(slot_of(item - 4), 0, 13)
            s = jnp.clip(slot - d, 0, 6)

            @pl.when((item > 0) & (flags[d, s] > 0))
            def _():
                act(d, r, slot)

            return code // 16

        lax.fori_loop(0, MOST, one, code)

    sums(0).start()
    for copy in innovations:
        copy.start()

    def fetch(d, carry):
        each(d, lambda d, r, slot: weights(d, r).start())

        @pl.when(d > 0)
        def _():
            sums(d).start()

        return carry

    lax.fori_loop(0, 8, fetch, 0)
    for copy in innovations:
        copy.wait()

    def add(d, r, slot):
        weights(d, r).wait()
        rows = jnp.concatenate([inn[slot, m] for m in range(8)], axis=1)
        total[d] += jnp.dot(gains[d, r], rows, preferred_element_type=jnp.float32)

    def close(d, carry):
        sums(d).wait()
        each(d, add)
        result(d).start()
        return carry

    lax.fori_loop(0, 8, close, 0)
    for d in range(8):
        result(d).wait()


def closing(in_radius, total, late, oi):
    used = len({e for others in LATE for e in others})
    return pl.pallas_call(
        closing_kernel,
        out_shape=jax.ShapeDtypeStruct((8, 256, 1024), jnp.float32),
        in_specs=[SMEM, HBM, HBM, HBM],
        out_specs=HBM,
        scratch_shapes=[
            pltpu.VMEM((8, 256, 1024), jnp.float32),
            pltpu.VMEM((8, MOST, 256, 256), jnp.bfloat16),
            pltpu.VMEM((14, 8, 256, 128), jnp.bfloat16),
            DMA((used,)),
            DMA((8, MOST)),
            DMA((8,)),
            DMA((8,)),
        ],
        compiler_params=pltpu.CompilerParams(vmem_limit_bytes=56 << 20),
    )(in_radius, total, late, oi)


def on_device(*arrays):
    total, late, xo, oi = analysis(*arrays)
    return closing(arrays[-1], total, late, oi)


def solution(mesh):
    return jax.shard_map(
        on_device,
        mesh=mesh,
        in_specs=(
            P("dist", None, "mem"),
            P("dist", None, "mem"),
            P("dist", None),
            P(None, "dist", None),
            P("dist", None),
            P("dist"),
            P("dist", None),
        ),
        out_specs=P("dist", "mem", None),
        check_vma=False,
    )
```

```python
import jax
import jax.numpy as jnp
from jax import lax
from jax.experimental import pallas as pl
from jax.experimental.pallas import tpu as pltpu
from jax.sharding import PartitionSpec as P

MESH = pl.DeviceIdType.MESH
HBM = pl.BlockSpec(memory_space=pltpu.HBM)
VMEM = pl.BlockSpec(memory_space=pltpu.VMEM)
SMEM = pl.BlockSpec(memory_space=pltpu.SMEM)
DMA = pltpu.SemaphoreType.DMA
RADIUS = 3
REACH = 2.5
UNITS = 16
LAG = 2
FAR_FIRST = (6, 2, 5, 7, 4, 1, 3)
STEPS = 22
OWN_USED = 14
NODE_TURN = (1, 0, 2, 3, 4, 5, 6, 7)


def column(*pairs):
    return sum(((e + 3) * 8 + d) * 128 ** i for i, (e, d) in enumerate(pairs))


GAIN_FIRST = 8
GAIN_TABLE = (
    column((0, 0), (0, 1), (1, 0), (1, 1)),
    column((0, 2), (1, 2), (2, 0), (2, 1)),
    column((2, 2), (3, 0), (3, 1), (3, 2)),
    column((0, 3), (1, 3), (-1, 0), (-1, 1)),
    column((-1, 2), (2, 3), (4, 1), (4, 2)),
    column((1, 4), (2, 4), (-2, 0), (-2, 1)),
    column((5, 2), (5, 3), (5, 4), (4, 3)),
    column((2, 5), (6, 3), (6, 4), (6, 5)),
    column((-3, 0), (5, 5), (4, 4), (4, 5)),
    column((7, 4), (7, 5), (7, 6), (6, 6)),
    column((8, 5), (8, 6), (5, 6), (9, 6)),
    column((7, 7), (6, 7), (8, 7), (5, 7)),
    column((9, 7), (4, 6), (4, 7), (10, 7)),
    column((3, 3), (3, 4), (3, 5), (3, 6)),
)
INC_FIRST = 12
INC_TABLE = (
    column((0, 0), (0, 1), (0, 2), (0, 3)),
    0,
    column((1, 0), (1, 1), (1, 2), (1, 3)),
    0,
    column((1, 4), (2, 0), (2, 1), (2, 2)),
    column((-1, 0), (-1, 1), (-1, 2), (2, 3)),
    column((2, 4), (2, 5), (-2, 0), (-2, 1)),
    column((7, 4), (7, 5), (7, 6), (7, 7)),
    column((6, 3), (6, 4), (6, 5), (6, 6)),
)
LATE = (
    (-3, 3,),
    (3, 4,),
    (3, 4, 5,),
    (3, 4, 5,),
    (3, 4, 5,),
    (3, 4, 5, 8,),
    (3, 4, 5, 8, 9,),
    (4, 5, 6, 8, 9, 10,),
)


LAST_GAINS = ((3, 3), (3, 4), (3, 5), (3, 6))
MOST = max(len(others) for others in LATE)


def analysis_kernel(
    anom, innov, node_h, count_h, pos_h, var_h, flags, out, late, xo, oi,
    held, seen, meta, node, count, pos, var, cols, xs, obs, inn, gains, total, inv, spot,
    a_s, a_r, g_s, g_r, h_s, h_r, m_s, m_r, l_s, p_s, w_s, v_s, x_s, o_s, f_s,
):
    di, j = lax.axis_index("dist"), lax.axis_index("mem")
    core = lax.rem(di, 2)
    zl, y = j // 4, lax.rem(j, 4)

    def mem_of(z, row):
        return z * 4 + lax.rem(row + 8, 4)

    def district(q):
        return q + core * (7 - 2 * q)

    small = [
        pltpu.make_async_copy(node_h, node, l_s.at[0]),
        pltpu.make_async_copy(count_h, count, l_s.at[1]),
        pltpu.make_async_copy(pos_h, pos, l_s.at[2]),
        pltpu.make_async_copy(var_h, var, l_s.at[3]),
    ]
    for copy in small:
        copy.start()

    def load(n):
        return pltpu.make_async_copy(anom.at[district(n)], held.at[lax.rem(n, 2)], p_s.at[lax.rem(n, 2)])

    load(0).start()
    load(1).start()
    take_x = pltpu.make_async_copy(anom.at[:, pl.ds(pl.multiple_of(j * 256, 256), 256), :], xs.at[:, j], l_s.at[4])
    take_innov = pltpu.make_async_copy(innov, inn.at[pl.ds(3, 8), j], l_s.at[5])
    own_x = pltpu.make_async_copy(xs.at[:, j], xo.at[:, j], l_s.at[4])
    own_innov = pltpu.make_async_copy(inn.at[pl.ds(3, 8), j], oi.at[1, pl.ds(3, 8), j], l_s.at[5])
    take_x.start()
    take_innov.start()

    flip = mem_of(1 - zl, y)
    other = di + 1 - 2 * core
    remote = lax.rem(di + 15 + 2 * core, 16)
    barrier = pltpu.get_barrier_semaphore()
    for k in range(1, 8):
        pl.semaphore_signal(barrier, inc=1, device_id={"dist": di, "mem": lax.rem(j + k, 8)}, device_id_type=MESH)
    pl.semaphore_signal(barrier, inc=1, device_id={"dist": other, "mem": j}, device_id_type=MESH)
    pl.semaphore_signal(barrier, inc=1, device_id={"dist": remote, "mem": flip}, device_id_type=MESH)
    for d in range(8):
        total[d] = jnp.zeros((256, 1024), jnp.float32)
    pl.semaphore_wait(barrier, 9)

    def remote_copy(source, target, send, recv, dist, mem):
        return pltpu.make_async_remote_copy(
            src_ref=source, dst_ref=target, send_sem=send, recv_sem=recv,
            device_id={"dist": dist, "mem": mem}, device_id_type=MESH)

    def spread_nodes(k, q):
        d = district(q)
        target = mem_of(lax.rem(zl + k // 4, 2), y + k % 4)
        return remote_copy(
            anom.at[d, pl.ds(pl.multiple_of(target * 256, 256), 256), :], xo.at[d, j],
            a_s.at[k - 1, q], a_r.at[k - 1, q], di, target)

    def unit(u):
        middle = (u >= 5) & (u < 11)
        odd = lax.rem(u, 2)
        kind = jnp.where(middle, odd, jnp.where(u < 5, 0, 1))
        q = jnp.where(middle, jnp.where(odd == 1, (u - 5) // 2, 2 + u // 2), jnp.where(u < 5, u, 18 - u))
        return kind, q, district(q), 1 - 2 * lax.rem(u, 2), lax.rem(u, 3) == 2

    def edge_copy(u, edge, source, block, mem):
        return remote_copy(source, block, g_s.at[edge, u], g_r.at[edge, u], di, mem)

    def forward(u, edge):
        kind, q, d, s, three = unit(u)
        here, there = zl, 1 - zl
        from_, to = {
            3: (mem_of(here, y - s), flip),
            4: (mem_of(here, y + s), jnp.where(three, flip, mem_of(here, y - s))),
            5: (jnp.where(three, mem_of(here, y - s), flip), jnp.where(three, mem_of(here, y + s), mem_of(here, y - s))),
            6: (jnp.where(three, mem_of(there, y + s), mem_of(there, y - s)),
                jnp.where(three, mem_of(here, y - s), mem_of(here, y + s))),
        }[edge]
        block = oi.at[kind, 3 + d, from_]
        return edge_copy(u, edge, block, block, to)

    def gathered(u, edge):
        kind, q, d, s, three = unit(u)
        here, there = zl, 1 - zl
        from_ = (
            mem_of(here, y - s),
            mem_of(here, y + s),
            flip,
            mem_of(there, y - s),
            jnp.where(three, mem_of(there, y + s), mem_of(here, y + 2)),
            jnp.where(three, mem_of(here, y + 2), mem_of(there, y + s)),
            mem_of(there, y + 2),
        )[edge]
        block = oi.at[kind, 3 + d, from_]
        return edge_copy(u, edge, block, block, flip)

    def halo(u):
        kind, q, d, s, three = unit(u)
        near = q >= 5
        slot = jnp.where(d >= 5, d - 5, 11 + d)
        index = jnp.where(near, q - 2, q)
        return remote_copy(
            oi.at[kind, 3 + d], oi.at[kind, slot], h_s.at[kind, index], h_r.at[kind, index],
            jnp.where(near, other, remote), jnp.where(near, j, flip))

    def halo_in(kind, index):
        slot = jnp.where(core == 0, jnp.where(index < 3, 2 - index, 16 - index), jnp.where(index < 3, 11 + index, index - 3))
        return remote_copy(oi.at[kind, slot], oi.at[kind, slot], h_s.at[kind, index], h_r.at[kind, index], other, j)

    def has_halo(u):
        q = unit(u)[1]
        return (q < 3) | (q >= 5)

    def own_seen(d):
        return pltpu.make_async_copy(seen.at[d], oi.at[0, 3 + d, j], w_s.at[d])

    for k in FAR_FIRST[:3]:
        spread_nodes(k, NODE_TURN[0]).start()
    for copy in small + [take_x, take_innov]:
        copy.wait()
    own_x.start()
    own_innov.start()
    slot8 = lax.broadcasted_iota(jnp.int32, (256, 8), 0)
    cols[...] = jnp.where(slot8 < count[...], node[...].T, -1)
    xy = pos[:, pl.ds(pl.multiple_of(j * 256, 256), 256)].astype(jnp.float32).T
    for d in range(8):
        for axis in range(2):
            spot[axis, d] = jnp.broadcast_to(xy[:, 8 * axis + d:8 * axis + d + 1], (256, 128))

    def observe(q):
        d, n = district(q), q
        load(n).wait()
        lane = lax.broadcasted_iota(jnp.int32, (256, 8), 1)
        which = jnp.sum(jnp.where(lane == d, cols[...], 0), axis=1, keepdims=True)
        hot = jnp.where(lax.broadcasted_iota(jnp.int32, (256, 2048), 1) == which, 1.0, 0.0).astype(jnp.bfloat16)
        rows = jnp.dot(hot, held[lax.rem(n, 2)], preferred_element_type=jnp.float32)
        seen[d] = rows.astype(jnp.bfloat16)
        spots = lax.dot_general(pos[...], hot, (((1,), (1,)), ((), ())), preferred_element_type=jnp.float32)
        row16 = lax.broadcasted_iota(jnp.int32, (16, 256), 0)
        row8 = lax.broadcasted_iota(jnp.int32, (8, 256), 0)
        sx = jnp.sum(jnp.where(row16 == d, spots, 0.0), axis=0, keepdims=True)
        sy = jnp.sum(jnp.where(row16 == d + 8, spots, 0.0), axis=0, keepdims=True)
        sv = jnp.sum(jnp.where(row8 == d, var[...].astype(jnp.float32), 0.0), axis=0, keepdims=True)
        meta[3 + d] = jnp.where(row8 == 0, sx, jnp.where(row8 == 1, sy, jnp.where(row8 == 2, sv, 0.0)))

        @pl.when(n < 6)
        def _():
            load(n + 2).start()

        own_seen(d).start()

    far_meta = remote_copy(
        meta.at[pl.ds(3 + 5 * core, 3)], meta.at[pl.ds(11 - 11 * core, 3)], m_s.at[0], m_r.at[0], remote, flip)
    near_meta = remote_copy(
        meta.at[pl.ds(8 - 5 * core, 3)], meta.at[pl.ds(11 * core, 3)], m_s.at[1], m_r.at[1], other, j)

    def slot_of(qe):
        return 3 + qe + core * (7 - 2 * qe)

    def bring(kind, slot, which):
        @pl.when(kind == 0)
        def _():
            pltpu.make_async_copy(oi.at[0, slot], obs.at[slot], v_s.at[which]).start()

        @pl.when(kind == 1)
        def _():
            pltpu.make_async_copy(oi.at[1, slot], inn.at[slot], v_s.at[which]).start()

    def brought(kind, slot, which):
        @pl.when(kind == 0)
        def _():
            pltpu.make_async_copy(oi.at[0, slot], obs.at[slot], v_s.at[which]).wait()
            square = jnp.zeros((256, 128), jnp.float32)
            for m in range(8):
                part = obs[slot, m].astype(jnp.float32)
                square = square + part * part
            square = jnp.sum(square.T, axis=0, keepdims=True)
            inv[pl.ds(slot, 1)] = 1.0 / (square + 1023.0 * meta[slot, 2:3])

        @pl.when(kind == 1)
        def _():
            pltpu.make_async_copy(oi.at[1, slot], inn.at[slot], v_s.at[which]).wait()

    def own_event(t, act):
        u = t - 3 * LAG

        @pl.when((u >= 0) & (u < OWN_USED))
        def _():
            kind, q, d, s, three = unit(u)
            act(kind, 3 + d, 0)

    def near_event(t, act, first):
        u = t - 3 * LAG - 1

        @pl.when((u == 6) | (u == 8) | ((u >= 10) & (u < 14)))
        def _():
            kind, q, d, s, three = unit(u)
            if first:
                halo_in(kind, q - 2).wait_recv()
            act(kind, slot_of(15 - q), 1)

    def far_event(t, act, first):
        early = t < 15
        i = jnp.where(early, t - 10, t - 15) // 2

        @pl.when((t == 10) | (t == 12) | (t == 14) | (t == 15) | (t == 17) | (t == 19))
        def _():
            kind = jnp.where(early, 0, 1)
            if first:
                halo_in(kind, i).wait_recv()
            act(kind, slot_of(-1 - i), 2)

    def nodes_copy(q):
        return pltpu.make_async_copy(xo.at[district(q)], xs.at[district(q)], x_s)

    def nodes_turn(t):
        turn = t // 2 - 2
        return (turn >= 0) & (turn < 8), jnp.where(turn < 2, 1 - turn, turn)

    def nodes_arrive(t):
        due, q = nodes_turn(t)

        @pl.when(t == 4)
        def _():
            own_x.wait()

        @pl.when(due & (lax.rem(t, 2) == 0))
        def _():
            d = district(q)
            for k in range(1, 8):
                source = mem_of(lax.rem(zl + k // 4, 2), y + 4 - k % 4)
                block = xo.at[d, source]
                remote_copy(block, block, a_s.at[k - 1, q], a_r.at[k - 1, q], di, flip).wait_recv()
            nodes_copy(q).start()

    def nodes_ready(t):
        due, q = nodes_turn(t)

        @pl.when(due & (lax.rem(t, 2) == 1))
        def _():
            nodes_copy(q).wait()

    def tasks(t, table, first):
        code = jnp.int32(0)
        for i, word in enumerate(table):
            if word:
                code = jnp.where(t == first + i, word, code)
        return code

    def places(code, i):
        item = lax.rem(code // (128 ** i), 128)
        d, slot = district(lax.rem(item, 8)), slot_of(item // 8 - 3)
        return d, slot, slot - d

    def joined(ref, index):
        return jnp.concatenate([ref[index, m] for m in range(8)], axis=1)

    def gain_block(t, part):
        code = tasks(t, GAIN_TABLE, GAIN_FIRST)

        @pl.when((t >= GAIN_FIRST) & (t < GAIN_FIRST + len(GAIN_TABLE)))
        def _():
            for i in part:
                d, slot, s = places(code, i)
                cov = lax.dot_general(joined(xs, d), joined(obs, slot), (((1,), (1,)), ((), ())), preferred_element_type=jnp.float32)
                row = inv[pl.ds(slot, 1)] * flags[d, s].astype(jnp.float32)
                node_x, node_y = spot[0, d], spot[1, d]
                weight = taper(
                    jnp.concatenate([node_x, node_x], axis=1), jnp.concatenate([node_y, node_y], axis=1),
                    meta[slot], (s - RADIUS).astype(jnp.float32))
                gains[d, s] = (weight * cov * row).astype(jnp.bfloat16)

    def increment_block(t):
        code = tasks(t, INC_TABLE, INC_FIRST)

        @pl.when(code > 0)
        def _():
            for i in range(4):
                d, slot, s = places(code, i)
                total[d] += jnp.dot(gains[d, s], joined(inn, slot), preferred_element_type=jnp.float32)

    def hand_over(last):
        copies = []
        for q, others in enumerate(LATE):
            for r, e in enumerate(others):
                if ((e, q) in LAST_GAINS) != last:
                    continue
                d = district(q)
                copies.append(pltpu.make_async_copy(gains.at[d, slot_of(e) - d], late.at[d, r], f_s.at[q, r]))
        return copies

    def finish(q):
        d = district(q)
        return pltpu.make_async_copy(total.at[d], out.at[d], o_s.at[q])

    def step(t, carry):
        @pl.when(t < UNITS)
        def _():
            kind, q, d, s, three = unit(t)
            targets = (mem_of(zl, y + s), mem_of(zl, y - s), flip)

            @pl.when(kind == 0)
            def _():
                observe(q)
                for edge in range(3):
                    edge_copy(t, edge, seen.at[d], oi.at[0, 3 + d, j], targets[edge]).start()

            @pl.when(kind == 1)
            def _():
                for edge in range(3):
                    edge_copy(t, edge, innov.at[d], oi.at[1, 3 + d, j], targets[edge]).start()

        @pl.when(t == 3)
        def _():
            far_meta.start()

        @pl.when(t == 9)
        def _():
            far_meta.wait_recv()

        @pl.when(t == 11)
        def _():
            near_meta.start()

        @pl.when(t == 13)
        def _():
            near_meta.wait_recv()


        own_event(t - 1, brought)
        near_event(t - 1, brought, False)
        far_event(t - 1, brought, False)
        nodes_ready(t)

        u = t - LAG

        @pl.when((u >= 0) & (u < UNITS))
        def _():
            for edge in range(3):
                gathered(u, edge).wait_recv()
                forward(u, edge + 3).start()

        v = t - 2 * LAG

        @pl.when((v >= 0) & (v < UNITS))
        def _():
            gathered_last(v, True)
            forward(v, 6).start()

        @pl.when(t == STEPS - 1)
        def _():
            for copy in hand_over(False):
                copy.start()
            for q in range(8):
                finish(q).start()

        turn = t // 2
        place = jnp.where(turn < 2, 1 - turn, turn)

        @pl.when((t >= 1) & (t < 16) & (lax.rem(t, 2) == 0))
        def _():
            for k in FAR_FIRST[:3]:
                spread_nodes(k, place).start()

        @pl.when((t < 16) & (lax.rem(t, 2) == 1))
        def _():
            for k in FAR_FIRST[3:]:
                spread_nodes(k, place).start()

        w = t - 3 * LAG

        @pl.when((w >= 0) & (w < UNITS))
        def _():
            gathered_last(w, False)
            gathered(w, 5).wait_recv()
            gathered(w, 6).wait_recv()
            kind, q, d, s, three = unit(w)

            @pl.when(kind == 0)
            def _():
                own_seen(d).wait()

            @pl.when(w == 3)
            def _():
                own_innov.wait()

            @pl.when(has_halo(w))
            def _():
                halo(w).start()

        own_event(t, bring)
        near_event(t, bring, True)
        far_event(t, bring, True)
        nodes_arrive(t)
        gain_block(t, (0, 1, 2, 3))
        increment_block(t)
        return carry

    def gathered_last(u, first):
        three = unit(u)[4]
        take4 = three if first else jnp.logical_not(three)

        @pl.when(take4)
        def _():
            gathered(u, 4).wait_recv()

        @pl.when(jnp.logical_not(take4))
        def _():
            gathered(u, 3).wait_recv()

    lax.fori_loop(0, STEPS, step, 0)
    for copy in hand_over(True):
        copy.start()

    def drain(u, carry):
        for edge in range(7):
            gathered(u, edge).wait_send()

        @pl.when(has_halo(u))
        def _():
            halo(u).wait_send()

        return carry

    lax.fori_loop(0, UNITS, drain, 0)

    def drain_nodes(q, carry):
        for k in range(1, 8):
            spread_nodes(k, q).wait_send()
        return carry

    lax.fori_loop(0, 8, drain_nodes, 0)
    far_meta.wait_send()
    near_meta.wait_send()
    for q in range(8):
        finish(q).wait()
    for copy in hand_over(False) + hand_over(True):
        copy.wait()


def taper(node_x, node_y, meta, shift):
    dx = (meta[0:1] + shift) - node_x
    dy = meta[1:2] - node_y
    square = jnp.maximum((dx * dx + dy * dy) * (1.0 / (REACH * REACH)), 1e-30)
    root = lax.rsqrt(square)
    z = square * root
    inner = (((-0.25 * z + 0.5) * z + 0.625) * z - 5.0 / 3.0) * square + 1.0
    left = jnp.maximum(2.0 - z, 0.0)
    left = left * left
    outer = (left * left) * (z * (1.0 / 12.0) + (1.0 / 6.0) - root * (1.0 / 24.0))
    return jnp.where(z < 1.0, inner, outer)


def analysis(anomalies, innovations, obs_var, node_pos, obs_node, obs_count, in_radius):
    bf16, f32 = jnp.bfloat16, jnp.float32
    return pl.pallas_call(
        analysis_kernel,
        out_shape=(
            jax.ShapeDtypeStruct((8, 256, 1024), f32),
            jax.ShapeDtypeStruct((8, MOST, 256, 256), bf16),
            jax.ShapeDtypeStruct((8, 8, 256, 128), bf16),
            jax.ShapeDtypeStruct((2, 14, 8, 256, 128), bf16),
        ),
        in_specs=[HBM] * 6 + [SMEM],
        out_specs=(HBM,) * 4,
        scratch_shapes=[
            pltpu.VMEM((2, 2048, 128), bf16),
            pltpu.VMEM((8, 256, 128), bf16),
            pltpu.VMEM((14, 8, 256), f32),
            pltpu.VMEM((8, 256), jnp.int32),
            pltpu.VMEM((1, 8), jnp.int32),
            pltpu.VMEM((16, 2048), bf16),
            pltpu.VMEM((8, 256), bf16),
            pltpu.VMEM((256, 8), jnp.int32),
            pltpu.VMEM((8, 8, 256, 128), bf16),
            pltpu.VMEM((14, 8, 256, 128), bf16),
            pltpu.VMEM((14, 8, 256, 128), bf16),
            pltpu.VMEM((8, 7, 256, 256), bf16),
            pltpu.VMEM((8, 256, 1024), f32),
            pltpu.VMEM((14, 256), f32),
            pltpu.VMEM((2, 8, 256, 128), f32),
            DMA((7, 8)), DMA((7, 8)), DMA((7, UNITS)), DMA((7, UNITS)), DMA((2, 6)), DMA((2, 6)), DMA((2,)), DMA((2,)),
            DMA((6,)), DMA((2,)), DMA((8,)), DMA((3,)), DMA, DMA((8,)), DMA((8, MOST)),
        ],
        compiler_params=pltpu.CompilerParams(collective_id=0, has_side_effects=True, vmem_limit_bytes=58 << 20),
    )(anomalies, innovations, obs_node, obs_count.reshape(1, 8), node_pos.reshape(16, 2048), obs_var, in_radius)


def closing_kernel(flags, total_h, late_h, oi, out, total, gains, inn, i_s, g_s, t_s, o_s):
    core = lax.rem(lax.axis_index("dist"), 2)

    def slot_of(qe):
        return 3 + qe + core * (7 - 2 * qe)

    used = sorted({e for others in LATE for e in others})
    first = [min(place for place, others in enumerate(LATE) if e in others) for e in used]

    def district(q):
        return q + core * (7 - 2 * q)

    wanted = [
        sum(flags[district(place), slot_of(e) - district(place)] for place, others in enumerate(LATE) if e in others)
        for e in used]

    def innovations(q, act):
        for i, e in enumerate(used):
            @pl.when((q == first[i]) & (wanted[i] > 0))
            def _():
                act(pltpu.make_async_copy(oi.at[1, slot_of(e)], inn.at[slot_of(e)], i_s.at[i]))

    def sums(d):
        return pltpu.make_async_copy(total_h.at[d], total.at[d], t_s.at[d])

    def result(d):
        return pltpu.make_async_copy(total.at[d], out.at[d], o_s.at[d])

    def weights(d, r):
        return pltpu.make_async_copy(late_h.at[d, r], gains.at[d, r], g_s.at[d, r])

    def each(q, act):
        d = district(q)
        code = jnp.int32(0)
        for place, others in enumerate(LATE):
            code = jnp.where(q == place, sum((e + 4) * 16 ** r for r, e in enumerate(others)), code)

        def one(r, code):
            item = lax.rem(code, 16)
            slot = jnp.clip(slot_of(item - 4), 0, 13)
            s = jnp.clip(slot - d, 0, 6)

            @pl.when((item > 0) & (flags[d, s] > 0))
            def _():
                act(d, r, slot)

            return code // 16

        lax.fori_loop(0, MOST, one, code)

    def fetch(q, carry):
        sums(district(q)).start()
        innovations(q, lambda copy: copy.start())
        each(q, lambda d, r, slot: weights(d, r).start())
        return carry

    lax.fori_loop(0, 8, fetch, 0)

    def add(d, r, slot):
        weights(d, r).wait()
        rows = jnp.concatenate([inn[slot, m] for m in range(8)], axis=1)
        total[d] += jnp.dot(gains[d, r], rows, preferred_element_type=jnp.float32)

    def close(q, carry):
        sums(district(q)).wait()
        innovations(q, lambda copy: copy.wait())
        each(q, add)
        result(district(q)).start()
        return carry

    lax.fori_loop(0, 8, close, 0)
    for d in range(8):
        result(d).wait()


def closing(in_radius, total, late, oi):
    used = len({e for others in LATE for e in others})
    return pl.pallas_call(
        closing_kernel,
        out_shape=jax.ShapeDtypeStruct((8, 256, 1024), jnp.float32),
        in_specs=[SMEM, HBM, HBM, HBM],
        out_specs=HBM,
        scratch_shapes=[
            pltpu.VMEM((8, 256, 1024), jnp.float32),
            pltpu.VMEM((8, MOST, 256, 256), jnp.bfloat16),
            pltpu.VMEM((14, 8, 256, 128), jnp.bfloat16),
            DMA((used,)),
            DMA((8, MOST)),
            DMA((8,)),
            DMA((8,)),
        ],
        compiler_params=pltpu.CompilerParams(vmem_limit_bytes=56 << 20),
    )(in_radius, total, late, oi)


def on_device(*arrays):
    total, late, xo, oi = analysis(*arrays)
    return closing(arrays[-1], total, late, oi)


def solution(mesh):
    return jax.shard_map(
        on_device,
        mesh=mesh,
        in_specs=(
            P("dist", None, "mem"),
            P("dist", None, "mem"),
            P("dist", None),
            P(None, "dist", None),
            P("dist", None),
            P("dist"),
            P("dist", None),
        ),
        out_specs=P("dist", "mem", None),
        check_vma=False,
    )
```

```python
import jax
import jax.numpy as jnp
from jax import lax
from jax.experimental import pallas as pl
from jax.experimental.pallas import tpu as pltpu
from jax.sharding import PartitionSpec as P

MESH = pl.DeviceIdType.MESH
HBM = pl.BlockSpec(memory_space=pltpu.HBM)
VMEM = pl.BlockSpec(memory_space=pltpu.VMEM)
SMEM = pl.BlockSpec(memory_space=pltpu.SMEM)
DMA = pltpu.SemaphoreType.DMA
RADIUS = 3
REACH = 2.5
UNITS = 16
LAG = 2
FAR_FIRST = (6, 2, 5, 7, 4, 1, 3)
STEPS = 22
OWN_USED = 14
NODE_TURN = (1, 0, 2, 3, 4, 5, 6, 7)


def column(*pairs):
    return sum(((e + 3) * 8 + d) * 128 ** i for i, (e, d) in enumerate(pairs))


GAIN_FIRST = 8
GAIN_TABLE = (
    column((0, 0), (0, 1), (1, 0), (1, 1)),
    column((0, 2), (1, 2), (2, 0), (2, 1)),
    column((2, 2), (3, 0), (3, 1), (3, 2)),
    column((0, 3), (1, 3), (-1, 0), (-1, 1)),
    column((-1, 2), (2, 3), (4, 1), (4, 2)),
    column((1, 4), (2, 4), (-2, 0), (-2, 1)),
    column((5, 2), (5, 3), (5, 4), (4, 3)),
    column((2, 5), (6, 3), (6, 4), (6, 5)),
    column((-3, 0), (5, 5), (4, 4), (4, 5)),
    column((7, 4), (7, 5), (7, 6), (6, 6)),
    column((8, 5), (8, 6), (5, 6), (9, 6)),
    column((7, 7), (6, 7), (8, 7), (5, 7)),
    column((9, 7), (4, 6), (4, 7), (10, 7)),
    column((3, 3), (3, 4), (3, 5), (3, 6)),
)
INC_FIRST = 12
INC_TABLE = (
    column((0, 0), (0, 1), (0, 2), (0, 3)),
    0,
    column((1, 0), (1, 1), (1, 2), (1, 3)),
    0,
    column((1, 4), (2, 0), (2, 1), (2, 2)),
    column((-1, 0), (-1, 1), (-1, 2), (2, 3)),
    column((2, 4), (2, 5), (-2, 0), (-2, 1)),
    column((7, 4), (7, 5), (7, 6), (7, 7)),
    column((6, 3), (6, 4), (6, 5), (6, 6)),
)
LATE = (
    (-3, 3,),
    (3, 4,),
    (3, 4, 5,),
    (3, 4, 5,),
    (3, 4, 5,),
    (3, 4, 5, 8,),
    (3, 4, 5, 8, 9,),
    (4, 5, 6, 8, 9, 10,),
)


LAST_GAINS = ((3, 3), (3, 4), (3, 5), (3, 6))
MOST = max(len(others) for others in LATE)


def analysis_kernel(
    anom, innov, node_h, count_h, pos_h, var_h, flags, out, late, xo, oi,
    held, seen, meta, node, count, pos, var, cols, xs, obs, inn, gains, total, inv, spot,
    a_s, a_r, g_s, g_r, h_s, h_r, m_s, m_r, l_s, p_s, w_s, v_s, x_s, o_s, f_s,
):
    di, j = lax.axis_index("dist"), lax.axis_index("mem")
    core = lax.rem(di, 2)
    zl, y = j // 4, lax.rem(j, 4)

    def mem_of(z, row):
        return z * 4 + lax.rem(row + 8, 4)

    def district(q):
        return q + core * (7 - 2 * q)

    small = [
        pltpu.make_async_copy(node_h, node, l_s.at[0]),
        pltpu.make_async_copy(count_h, count, l_s.at[1]),
        pltpu.make_async_copy(pos_h, pos, l_s.at[2]),
        pltpu.make_async_copy(var_h, var, l_s.at[3]),
    ]
    for copy in small:
        copy.start()

    def load(n):
        return pltpu.make_async_copy(anom.at[district(n)], held.at[lax.rem(n, 2)], p_s.at[lax.rem(n, 2)])

    load(0).start()
    load(1).start()
    take_x = pltpu.make_async_copy(anom.at[:, pl.ds(pl.multiple_of(j * 256, 256), 256), :], xs.at[:, j], l_s.at[4])
    take_innov = pltpu.make_async_copy(innov, inn.at[pl.ds(3, 8), j], l_s.at[5])
    own_x = pltpu.make_async_copy(xs.at[:, j], xo.at[:, j], l_s.at[4])
    own_innov = pltpu.make_async_copy(inn.at[pl.ds(3, 8), j], oi.at[1, pl.ds(3, 8), j], l_s.at[5])
    take_x.start()
    take_innov.start()

    flip = mem_of(1 - zl, y)
    other = di + 1 - 2 * core
    remote = lax.rem(di + 15 + 2 * core, 16)
    barrier = pltpu.get_barrier_semaphore()
    for k in range(1, 8):
        pl.semaphore_signal(barrier, inc=1, device_id={"dist": di, "mem": lax.rem(j + k, 8)}, device_id_type=MESH)
    pl.semaphore_signal(barrier, inc=1, device_id={"dist": other, "mem": j}, device_id_type=MESH)
    pl.semaphore_signal(barrier, inc=1, device_id={"dist": remote, "mem": flip}, device_id_type=MESH)
    for d in range(8):
        total[d] = jnp.zeros((256, 1024), jnp.float32)
    pl.semaphore_wait(barrier, 9)

    def remote_copy(source, target, send, recv, dist, mem):
        return pltpu.make_async_remote_copy(
            src_ref=source, dst_ref=target, send_sem=send, recv_sem=recv,
            device_id={"dist": dist, "mem": mem}, device_id_type=MESH)

    def spread_nodes(k, q):
        d = district(q)
        target = mem_of(lax.rem(zl + k // 4, 2), y + k % 4)
        return remote_copy(
            anom.at[d, pl.ds(pl.multiple_of(target * 256, 256), 256), :], xo.at[d, j],
            a_s.at[k - 1, q], a_r.at[k - 1, q], di, target)

    def unit(u):
        middle = (u >= 5) & (u < 11)
        odd = lax.rem(u, 2)
        kind = jnp.where(middle, odd, jnp.where(u < 5, 0, 1))
        q = jnp.where(middle, jnp.where(odd == 1, (u - 5) // 2, 2 + u // 2), jnp.where(u < 5, u, 18 - u))
        return kind, q, district(q), 1 - 2 * lax.rem(u, 2), lax.rem(u, 3) == 2

    def edge_copy(u, edge, source, block, mem):
        return remote_copy(source, block, g_s.at[edge, u], g_r.at[edge, u], di, mem)

    def forward(u, edge):
        kind, q, d, s, three = unit(u)
        here, there = zl, 1 - zl
        from_, to = {
            3: (mem_of(here, y - s), flip),
            4: (mem_of(here, y + s), jnp.where(three, flip, mem_of(here, y - s))),
            5: (jnp.where(three, mem_of(here, y - s), flip), jnp.where(three, mem_of(here, y + s), mem_of(here, y - s))),
            6: (jnp.where(three, mem_of(there, y + s), mem_of(there, y - s)),
                jnp.where(three, mem_of(here, y - s), mem_of(here, y + s))),
        }[edge]
        block = oi.at[kind, 3 + d, from_]
        return edge_copy(u, edge, block, block, to)

    def gathered(u, edge):
        kind, q, d, s, three = unit(u)
        here, there = zl, 1 - zl
        from_ = (
            mem_of(here, y - s),
            mem_of(here, y + s),
            flip,
            mem_of(there, y - s),
            jnp.where(three, mem_of(there, y + s), mem_of(here, y + 2)),
            jnp.where(three, mem_of(here, y + 2), mem_of(there, y + s)),
            mem_of(there, y + 2),
        )[edge]
        block = oi.at[kind, 3 + d, from_]
        return edge_copy(u, edge, block, block, flip)

    def halo(u):
        kind, q, d, s, three = unit(u)
        near = q >= 5
        slot = jnp.where(d >= 5, d - 5, 11 + d)
        index = jnp.where(near, q - 2, q)
        return remote_copy(
            oi.at[kind, 3 + d], oi.at[kind, slot], h_s.at[kind, index], h_r.at[kind, index],
            jnp.where(near, other, remote), jnp.where(near, j, flip))

    def halo_in(kind, index):
        slot = jnp.where(core == 0, jnp.where(index < 3, 2 - index, 16 - index), jnp.where(index < 3, 11 + index, index - 3))
        return remote_copy(oi.at[kind, slot], oi.at[kind, slot], h_s.at[kind, index], h_r.at[kind, index], other, j)

    def has_halo(u):
        q = unit(u)[1]
        return (q < 3) | (q >= 5)

    def own_seen(d):
        return pltpu.make_async_copy(seen.at[d], oi.at[0, 3 + d, j], w_s.at[d])

    for k in FAR_FIRST[:3]:
        spread_nodes(k, NODE_TURN[0]).start()
    for copy in small + [take_x, take_innov]:
        copy.wait()
    own_x.start()
    own_innov.start()
    slot8 = lax.broadcasted_iota(jnp.int32, (256, 8), 0)
    cols[...] = jnp.where(slot8 < count[...], node[...].T, -1)
    xy = pos[:, pl.ds(pl.multiple_of(j * 256, 256), 256)].astype(jnp.float32).T
    for d in range(8):
        for axis in range(2):
            spot[axis, d] = jnp.broadcast_to(xy[:, 8 * axis + d:8 * axis + d + 1], (256, 128))

    def observe(q):
        d, n = district(q), q
        load(n).wait()
        lane = lax.broadcasted_iota(jnp.int32, (256, 8), 1)
        which = jnp.sum(jnp.where(lane == d, cols[...], 0), axis=1, keepdims=True)
        hot = jnp.where(lax.broadcasted_iota(jnp.int32, (256, 2048), 1) == which, 1.0, 0.0).astype(jnp.bfloat16)
        rows = jnp.dot(hot, held[lax.rem(n, 2)], preferred_element_type=jnp.float32)
        seen[d] = rows.astype(jnp.bfloat16)
        spots = lax.dot_general(pos[...], hot, (((1,), (1,)), ((), ())), preferred_element_type=jnp.float32)
        row16 = lax.broadcasted_iota(jnp.int32, (16, 256), 0)
        row8 = lax.broadcasted_iota(jnp.int32, (8, 256), 0)
        sx = jnp.sum(jnp.where(row16 == d, spots, 0.0), axis=0, keepdims=True)
        sy = jnp.sum(jnp.where(row16 == d + 8, spots, 0.0), axis=0, keepdims=True)
        sv = jnp.sum(jnp.where(row8 == d, var[...].astype(jnp.float32), 0.0), axis=0, keepdims=True)
        meta[3 + d] = jnp.where(row8 == 0, sx, jnp.where(row8 == 1, sy, jnp.where(row8 == 2, sv, 0.0)))

        @pl.when(n < 6)
        def _():
            load(n + 2).start()

        own_seen(d).start()

    far_meta = remote_copy(
        meta.at[pl.ds(3 + 5 * core, 3)], meta.at[pl.ds(11 - 11 * core, 3)], m_s.at[0], m_r.at[0], remote, flip)
    near_meta = remote_copy(
        meta.at[pl.ds(8 - 5 * core, 3)], meta.at[pl.ds(11 * core, 3)], m_s.at[1], m_r.at[1], other, j)

    def slot_of(qe):
        return 3 + qe + core * (7 - 2 * qe)

    def bring(kind, slot, which):
        @pl.when(kind == 0)
        def _():
            pltpu.make_async_copy(oi.at[0, slot], obs.at[slot], v_s.at[which]).start()

        @pl.when(kind == 1)
        def _():
            pltpu.make_async_copy(oi.at[1, slot], inn.at[slot], v_s.at[which]).start()

    def brought(kind, slot, which):
        @pl.when(kind == 0)
        def _():
            pltpu.make_async_copy(oi.at[0, slot], obs.at[slot], v_s.at[which]).wait()
            square = jnp.zeros((256, 128), jnp.float32)
            for m in range(8):
                part = obs[slot, m].astype(jnp.float32)
                square = square + part * part
            square = jnp.sum(square.T, axis=0, keepdims=True)
            inv[pl.ds(slot, 1)] = 1.0 / (square + 1023.0 * meta[slot, 2:3])

        @pl.when(kind == 1)
        def _():
            pltpu.make_async_copy(oi.at[1, slot], inn.at[slot], v_s.at[which]).wait()

    def own_event(t, act):
        u = t - 3 * LAG

        @pl.when((u >= 0) & (u < OWN_USED))
        def _():
            kind, q, d, s, three = unit(u)
            act(kind, 3 + d, 0)

    def near_event(t, act, first):
        u = t - 3 * LAG - 1

        @pl.when((u == 6) | (u == 8) | ((u >= 10) & (u < 14)))
        def _():
            kind, q, d, s, three = unit(u)
            if first:
                halo_in(kind, q - 2).wait_recv()
            act(kind, slot_of(15 - q), 1)

    def far_event(t, act, first):
        early = t < 15
        i = jnp.where(early, t - 10, t - 15) // 2

        @pl.when((t == 10) | (t == 12) | (t == 14) | (t == 15) | (t == 17) | (t == 19))
        def _():
            kind = jnp.where(early, 0, 1)
            if first:
                halo_in(kind, i).wait_recv()
            act(kind, slot_of(-1 - i), 2)

    def nodes_copy(q):
        return pltpu.make_async_copy(xo.at[district(q)], xs.at[district(q)], x_s)

    def nodes_turn(t):
        turn = t // 2 - 2
        return (turn >= 0) & (turn < 8), jnp.where(turn < 2, 1 - turn, turn)

    def nodes_arrive(t):
        due, q = nodes_turn(t)

        @pl.when(t == 4)
        def _():
            own_x.wait()

        @pl.when(due & (lax.rem(t, 2) == 0))
        def _():
            d = district(q)
            for k in range(1, 8):
                source = mem_of(lax.rem(zl + k // 4, 2), y + 4 - k % 4)
                block = xo.at[d, source]
                remote_copy(block, block, a_s.at[k - 1, q], a_r.at[k - 1, q], di, flip).wait_recv()
            nodes_copy(q).start()

    def nodes_ready(t):
        due, q = nodes_turn(t)

        @pl.when(due & (lax.rem(t, 2) == 1))
        def _():
            nodes_copy(q).wait()

    def tasks(t, table, first):
        code = jnp.int32(0)
        for i, word in enumerate(table):
            if word:
                code = jnp.where(t == first + i, word, code)
        return code

    def places(code, i):
        item = lax.rem(code // (128 ** i), 128)
        d, slot = district(lax.rem(item, 8)), slot_of(item // 8 - 3)
        return d, slot, slot - d

    def joined(ref, index):
        return jnp.concatenate([ref[index, m] for m in range(8)], axis=1)

    def gain_block(t, part):
        code = tasks(t, GAIN_TABLE, GAIN_FIRST)

        @pl.when((t >= GAIN_FIRST) & (t < GAIN_FIRST + len(GAIN_TABLE)))
        def _():
            for i in part:
                d, slot, s = places(code, i)
                cov = lax.dot_general(joined(xs, d), joined(obs, slot), (((1,), (1,)), ((), ())), preferred_element_type=jnp.float32)
                row = inv[pl.ds(slot, 1)] * flags[d, s].astype(jnp.float32)
                node_x, node_y = spot[0, d], spot[1, d]
                weight = taper(
                    jnp.concatenate([node_x, node_x], axis=1), jnp.concatenate([node_y, node_y], axis=1),
                    meta[slot], (s - RADIUS).astype(jnp.float32))
                gains[d, s] = (weight * cov * row).astype(jnp.bfloat16)

    def increment_block(t):
        code = tasks(t, INC_TABLE, INC_FIRST)

        @pl.when(code > 0)
        def _():
            for i in range(4):
                d, slot, s = places(code, i)
                total[d] += jnp.dot(gains[d, s], joined(inn, slot), preferred_element_type=jnp.float32)

    def hand_over(last):
        copies = []
        for q, others in enumerate(LATE):
            for r, e in enumerate(others):
                if ((e, q) in LAST_GAINS) != last:
                    continue
                d = district(q)
                copies.append(pltpu.make_async_copy(gains.at[d, slot_of(e) - d], late.at[d, r], f_s.at[q, r]))
        return copies

    def finish(q):
        d = district(q)
        return pltpu.make_async_copy(total.at[d], out.at[d], o_s.at[q])

    def step(t, carry):
        @pl.when(t < UNITS)
        def _():
            kind, q, d, s, three = unit(t)
            targets = (mem_of(zl, y + s), mem_of(zl, y - s), flip)

            @pl.when(kind == 0)
            def _():
                observe(q)
                for edge in (2, 0, 1):
                    edge_copy(t, edge, seen.at[d], oi.at[0, 3 + d, j], targets[edge]).start()

            @pl.when(kind == 1)
            def _():
                for edge in (2, 0, 1):
                    edge_copy(t, edge, innov.at[d], oi.at[1, 3 + d, j], targets[edge]).start()

        @pl.when(t == 3)
        def _():
            far_meta.start()

        @pl.when(t == 9)
        def _():
            far_meta.wait_recv()

        @pl.when(t == 11)
        def _():
            near_meta.start()

        @pl.when(t == 13)
        def _():
            near_meta.wait_recv()


        own_event(t - 1, brought)
        near_event(t - 1, brought, False)
        far_event(t - 1, brought, False)
        nodes_ready(t)

        u = t - LAG

        @pl.when((u >= 0) & (u < UNITS))
        def _():
            for edge in range(3):
                gathered(u, edge).wait_recv()
                forward(u, edge + 3).start()

        v = t - 2 * LAG

        @pl.when((v >= 0) & (v < UNITS))
        def _():
            gathered_last(v, True)
            forward(v, 6).start()

        @pl.when(t == STEPS - 1)
        def _():
            for copy in hand_over(False):
                copy.start()
            for q in range(8):
                finish(q).start()

        turn = t // 2
        place = jnp.where(turn < 2, 1 - turn, turn)

        @pl.when((t >= 1) & (t < 16) & (lax.rem(t, 2) == 0))
        def _():
            for k in FAR_FIRST[:3]:
                spread_nodes(k, place).start()

        @pl.when((t < 16) & (lax.rem(t, 2) == 1))
        def _():
            for k in FAR_FIRST[3:]:
                spread_nodes(k, place).start()

        w = t - 3 * LAG

        @pl.when((w >= 0) & (w < UNITS))
        def _():
            gathered_last(w, False)
            gathered(w, 5).wait_recv()
            gathered(w, 6).wait_recv()
            kind, q, d, s, three = unit(w)

            @pl.when(kind == 0)
            def _():
                own_seen(d).wait()

            @pl.when(w == 3)
            def _():
                own_innov.wait()

            @pl.when(has_halo(w))
            def _():
                halo(w).start()

        own_event(t, bring)
        near_event(t, bring, True)
        far_event(t, bring, True)
        nodes_arrive(t)
        gain_block(t, (0, 1, 2, 3))
        increment_block(t)
        return carry

    def gathered_last(u, first):
        three = unit(u)[4]
        take4 = three if first else jnp.logical_not(three)

        @pl.when(take4)
        def _():
            gathered(u, 4).wait_recv()

        @pl.when(jnp.logical_not(take4))
        def _():
            gathered(u, 3).wait_recv()

    lax.fori_loop(0, STEPS, step, 0)
    for copy in hand_over(True):
        copy.start()

    def drain(u, carry):
        for edge in range(7):
            gathered(u, edge).wait_send()

        @pl.when(has_halo(u))
        def _():
            halo(u).wait_send()

        return carry

    lax.fori_loop(0, UNITS, drain, 0)

    def drain_nodes(q, carry):
        for k in range(1, 8):
            spread_nodes(k, q).wait_send()
        return carry

    lax.fori_loop(0, 8, drain_nodes, 0)
    far_meta.wait_send()
    near_meta.wait_send()
    for q in range(8):
        finish(q).wait()
    for copy in hand_over(False) + hand_over(True):
        copy.wait()


def taper(node_x, node_y, meta, shift):
    dx = (meta[0:1] + shift) - node_x
    dy = meta[1:2] - node_y
    square = jnp.maximum((dx * dx + dy * dy) * (1.0 / (REACH * REACH)), 1e-30)
    root = lax.rsqrt(square)
    z = square * root
    inner = (((-0.25 * z + 0.5) * z + 0.625) * z - 5.0 / 3.0) * square + 1.0
    left = jnp.maximum(2.0 - z, 0.0)
    left = left * left
    outer = (left * left) * (z * (1.0 / 12.0) + (1.0 / 6.0) - root * (1.0 / 24.0))
    return jnp.where(z < 1.0, inner, outer)


def analysis(anomalies, innovations, obs_var, node_pos, obs_node, obs_count, in_radius):
    bf16, f32 = jnp.bfloat16, jnp.float32
    return pl.pallas_call(
        analysis_kernel,
        out_shape=(
            jax.ShapeDtypeStruct((8, 256, 1024), f32),
            jax.ShapeDtypeStruct((8, MOST, 256, 256), bf16),
            jax.ShapeDtypeStruct((8, 8, 256, 128), bf16),
            jax.ShapeDtypeStruct((2, 14, 8, 256, 128), bf16),
        ),
        in_specs=[HBM] * 6 + [SMEM],
        out_specs=(HBM,) * 4,
        scratch_shapes=[
            pltpu.VMEM((2, 2048, 128), bf16),
            pltpu.VMEM((8, 256, 128), bf16),
            pltpu.VMEM((14, 8, 256), f32),
            pltpu.VMEM((8, 256), jnp.int32),
            pltpu.VMEM((1, 8), jnp.int32),
            pltpu.VMEM((16, 2048), bf16),
            pltpu.VMEM((8, 256), bf16),
            pltpu.VMEM((256, 8), jnp.int32),
            pltpu.VMEM((8, 8, 256, 128), bf16),
            pltpu.VMEM((14, 8, 256, 128), bf16),
            pltpu.VMEM((14, 8, 256, 128), bf16),
            pltpu.VMEM((8, 7, 256, 256), bf16),
            pltpu.VMEM((8, 256, 1024), f32),
            pltpu.VMEM((14, 256), f32),
            pltpu.VMEM((2, 8, 256, 128), f32),
            DMA((7, 8)), DMA((7, 8)), DMA((7, UNITS)), DMA((7, UNITS)), DMA((2, 6)), DMA((2, 6)), DMA((2,)), DMA((2,)),
            DMA((6,)), DMA((2,)), DMA((8,)), DMA((3,)), DMA, DMA((8,)), DMA((8, MOST)),
        ],
        compiler_params=pltpu.CompilerParams(collective_id=0, has_side_effects=True, vmem_limit_bytes=58 << 20),
    )(anomalies, innovations, obs_node, obs_count.reshape(1, 8), node_pos.reshape(16, 2048), obs_var, in_radius)


def closing_kernel(flags, total_h, late_h, oi, out, total, gains, inn, i_s, g_s, t_s, o_s):
    core = lax.rem(lax.axis_index("dist"), 2)

    def slot_of(qe):
        return 3 + qe + core * (7 - 2 * qe)

    used = sorted({e for others in LATE for e in others})
    innovations = [
        pltpu.make_async_copy(oi.at[1, slot_of(e)], inn.at[slot_of(e)], i_s.at[i]) for i, e in enumerate(used)]

    def sums(d):
        return pltpu.make_async_copy(total_h.at[d], total.at[d], t_s.at[d])

    def result(d):
        return pltpu.make_async_copy(total.at[d], out.at[d], o_s.at[d])

    def weights(d, r):
        return pltpu.make_async_copy(late_h.at[d, r], gains.at[d, r], g_s.at[d, r])

    def each(d, act):
        q = d + core * (7 - 2 * d)
        code = jnp.int32(0)
        for place, others in enumerate(LATE):
            code = jnp.where(q == place, sum((e + 4) * 16 ** r for r, e in enumerate(others)), code)

        def one(r, code):
            item = lax.rem(code, 16)
            slot = jnp.clip(slot_of(item - 4), 0, 13)
            s = jnp.clip(slot - d, 0, 6)

            @pl.when((item > 0) & (flags[d, s] > 0))
            def _():
                act(d, r, slot)

            return code // 16

        lax.fori_loop(0, MOST, one, code)

    sums(0).start()
    for copy in innovations:
        copy.start()

    def fetch(d, carry):
        each(d, lambda d, r, slot: weights(d, r).start())

        @pl.when(d > 0)
        def _():
            sums(d).start()

        return carry

    lax.fori_loop(0, 8, fetch, 0)
    for copy in innovations:
        copy.wait()

    def add(d, r, slot):
        weights(d, r).wait()
        rows = jnp.concatenate([inn[slot, m] for m in range(8)], axis=1)
        total[d] += jnp.dot(gains[d, r], rows, preferred_element_type=jnp.float32)

    def close(d, carry):
        sums(d).wait()
        each(d, add)
        result(d).start()
        return carry

    lax.fori_loop(0, 8, close, 0)
    for d in range(8):
        result(d).wait()


def closing(in_radius, total, late, oi):
    used = len({e for others in LATE for e in others})
    return pl.pallas_call(
        closing_kernel,
        out_shape=jax.ShapeDtypeStruct((8, 256, 1024), jnp.float32),
        in_specs=[SMEM, HBM, HBM, HBM],
        out_specs=HBM,
        scratch_shapes=[
            pltpu.VMEM((8, 256, 1024), jnp.float32),
            pltpu.VMEM((8, MOST, 256, 256), jnp.bfloat16),
            pltpu.VMEM((14, 8, 256, 128), jnp.bfloat16),
            DMA((used,)),
            DMA((8, MOST)),
            DMA((8,)),
            DMA((8,)),
        ],
        compiler_params=pltpu.CompilerParams(vmem_limit_bytes=56 << 20),
    )(in_radius, total, late, oi)


def on_device(*arrays):
    total, late, xo, oi = analysis(*arrays)
    return closing(arrays[-1], total, late, oi)


def solution(mesh):
    return jax.shard_map(
        on_device,
        mesh=mesh,
        in_specs=(
            P("dist", None, "mem"),
            P("dist", None, "mem"),
            P("dist", None),
            P(None, "dist", None),
            P("dist", None),
            P("dist"),
            P("dist", None),
        ),
        out_specs=P("dist", "mem", None),
        check_vma=False,
    )
```
